32 devices in a mesh: tok: 16 (over z, x, core), head: 2 (over y).
Axes of the slice: x: 2, y: 2, z: 4, core: 2. Of those that a mesh axis runs over, the one named last changes fastest.
Arguments:
- query: bfloat16 [4096, 5120], P('tok', 'head'), may hold values from -8 to 8
- leaf_kv: bfloat16 [4096, 2048], P('tok', 'head'), may hold values from -6 to 6
- doc_kv: bfloat16 [512, 2048], P(('tok', 'head')), may hold values from -8 to 8
- grad_out: bfloat16 [4096, 5120], P('tok', 'head'), may hold values from -6 to 6
- block_parent: int32 [16], replicated, may hold values from 0 to 14, as said below
- leaf_block: int32 [16], replicated, may hold values from 0 to 15
- leaf_seg: int32 [16, 256], P('tok'), may hold values from 0 to 3, never falling along the last dimension, each value on 1 to 128 neighbouring positions
Outputs:
- query_grad: bfloat16 [4096, 5120], P('tok', 'head')
- leaf_kv_grad: bfloat16 [4096, 2048], P('tok', 'head')
- doc_kv_grad: bfloat16 [512, 2048], P(('tok', 'head'))
The draws below stay inside these ranges and needn't reach their ends.
Inputs may be any that keep to these rules, and one draw needn't show every extreme that they name: block_parent[0] = 0 and block_parent[b] < b for b >= 1, so the blocks form a tree in tree order with root block 0. `leaf_seg`: segment numbers never fall along a query block.
All inputs are finite; a program needn't handle non-finite values.
Results may differ from the reference program's by a relative error of at most 0.0081.
Values may be sent and summed in bfloat16 or wider, within the bound.
No kernel may reach another device: no remote copies, remote signals or barrier semaphores. Data moves between devices by JAX's collectives and lax.ppermute only.
A program may use at most 64 MiB of HBM per device.

```python
import math
import jax
import jax.numpy as jnp
import numpy as np
from jax import lax

QH = 40
KVH = 8
HD = 128
LEAF_DEV = 256
DOC_DEV = 32
NBLK = 16
QTOK = 4096
DOC = 512


def draw_query(key, part):
    base_key = jax.random.fold_in(key, 11)
    array_shape = (QTOK, QH * HD)
    values = jnp.clip(jax.random.normal(base_key, array_shape, jnp.float32), -6.0, 6.0)
    return values.astype(jnp.bfloat16)


def draw_doc_kv(key, part):
    base_key = jax.random.fold_in(key, 12)
    array_shape = (DOC, KVH * 2 * HD)
    values = jnp.clip(jax.random.normal(base_key, array_shape, jnp.float32), -6.0, 6.0)
    return values.astype(jnp.bfloat16)


def draw_block_parent(key, part):
    base_key = jax.random.fold_in(key, 21)
    coin_key, distant_key = jax.random.split(base_key)
    indices = jnp.arange(NBLK, dtype=jnp.int32)
    coin_flip = jax.random.randint(coin_key, (NBLK,), 0, 2, dtype=jnp.int32)
    distant = jax.random.randint(distant_key, (NBLK,), 0, 1048576, dtype=jnp.int32) % jnp.maximum(indices, 1)
    parent = jnp.where(coin_flip == 1, indices - 1, distant)
    parent = jnp.where(indices == 0, 0, parent)
    parent = jnp.where(indices == NBLK - 1, NBLK - 2, parent)
    return parent.astype(jnp.int32)


def plant(drawn, key, low, largest):
    extent = drawn.shape
    index_at = [jax.random.randint(jax.random.fold_in(key, axis), (), 0, extent[axis]) for axis in range(len(extent))]
    drawn = drawn.at[tuple(index_at)].set(low)
    longest = extent.index(max(extent))
    index_at[longest] = (index_at[longest] + 1) % extent[longest]
    return drawn.at[tuple(index_at)].set(largest)


def level_of(stream_key, shape, cuts, least, high):
    level = 1.0
    for dim, shards_of in cuts:
        steps = jax.random.uniform(jax.random.fold_in(jax.random.fold_in(stream_key, 6), dim), (shards_of,), jnp.float32, least / len(cuts), high / len(cuts))
        level = level * jnp.repeat(jnp.exp(steps), shape[dim] // shards_of).reshape((-1,) + (1,) * (len(shape) - 1 - dim))
    return level


def length_profile(count, total, limit, skew):
    weights = [(1 << 20) // math.isqrt(rank ** skew) + 1 for rank in range(2, count + 1)]
    surplus, given = total - limit - (count - 1), [1] * (count - 1)
    while surplus > 0:
        free = [i for i in range(count - 1) if given[i] < limit]
        whole, budget = sum([weights[i] for i in free]), surplus
        for i in free:
            more = min(limit - given[i], max(1, budget * weights[i] // whole), surplus)
            given[i] = given[i] + more
            surplus = surplus - more
    return np.array([limit] + given)


def ragged(key, number_of, total, most, slope):
    if number_of == 2:
        one = jax.random.randint(key, (), max(1, total - most), min(most, total - 1) + 1)
        return jnp.stack([one, total - one])
    tallies = jnp.asarray(length_profile(number_of, total, most, slope), jnp.int32)
    pairs = (number_of - 1) // 2
    donor, sink = tallies[1:1 + 2 * pairs:2], tallies[2:2 + 2 * pairs:2]
    room = jnp.minimum(donor - 1, most - sink)
    moved = jax.random.randint(jax.random.fold_in(key, 1), (pairs,), 0, 1 << 20) % (room + 1)
    tallies = tallies.at[1:1 + 2 * pairs:2].set(donor - moved).at[2:2 + 2 * pairs:2].set(sink + moved)
    return tallies[jax.random.permutation(jax.random.fold_in(key, 2), number_of)]


def centred(key, extent, scale, most, cuts=(), kind=jnp.bfloat16):
    entries = scale * jax.random.normal(key, extent, jnp.float32)
    if cuts:
        entries = entries * level_of(key, extent, cuts, -0.22, 0.18)
    return jnp.clip(entries, -most, most).astype(kind)


def setup_inputs(seed: int = 0) -> dict:
    keys = jax.random.split(jax.random.key(seed), 8)
    return {
        "query": draw_query(jax.random.fold_in(keys[7], 71), 0),
        "leaf_kv": centred(keys[1], (QTOK, KVH * 2 * HD), 1.0, 6.0, ((0, 16), (1, 2))),
        "doc_kv": draw_doc_kv(jax.random.fold_in(keys[7], 71), 0),
        "grad_out": centred(keys[3], (QTOK, QH * HD), 1.0, 6.0, ((0, 16), (1, 2))),
        "block_parent": draw_block_parent(jax.random.fold_in(keys[7], 71), 0),
        "leaf_block": plant(jax.random.randint(keys[5], (NBLK,), 0, NBLK), jax.random.fold_in(keys[5], 1), 0, NBLK - 1).astype(jnp.int32),
        "leaf_seg": jax.vmap(lambda own: jnp.searchsorted(jnp.cumsum(ragged(own, max(3, LEAF_DEV // 64), LEAF_DEV, LEAF_DEV // 2, 2)), jnp.arange(LEAF_DEV), side="right"))(jax.random.split(keys[6], NBLK)).reshape((NBLK, LEAF_DEV)).astype(jnp.int32),
    }


def reach_table(block_parent):
    nodes = block_parent.shape[0]
    indices = jnp.arange(nodes, dtype=jnp.int32)
    adjacency = ((block_parent[:, None] == indices[None, :]) | (indices[:, None] == indices[None, :])).astype(jnp.float32)
    for sweep_index in range(nodes.bit_length()):
        adjacency = jnp.minimum(jnp.dot(adjacency, adjacency, precision=lax.Precision.HIGHEST), 1.0)
    return adjacency


def held_bf16(values):
    return lax.optimization_barrier(values.astype(jnp.bfloat16)).astype(jnp.float32)


def reference(query, leaf_kv, doc_kv, grad_out, block_parent, leaf_block, leaf_seg):
    groups = QH // KVH
    score_scale = HD ** -0.5
    ancestors = reach_table(block_parent)
    doc_pairs = doc_kv.reshape(DOC, KVH, 2, HD).astype(jnp.float32)
    doc_keys = doc_pairs[:, :, 0]
    doc_values = doc_pairs[:, :, 1]
    positions = jnp.arange(LEAF_DEV, dtype=jnp.int32)

    def one_block(running, block_index):
        first_row = block_index * LEAF_DEV
        queries = lax.dynamic_slice_in_dim(query, first_row, LEAF_DEV, 0).reshape(LEAF_DEV, KVH, groups, HD).astype(jnp.float32)
        out_grads = lax.dynamic_slice_in_dim(grad_out, first_row, LEAF_DEV, 0).reshape(LEAF_DEV, KVH, groups, HD).astype(jnp.float32)
        leaf_pairs = lax.dynamic_slice_in_dim(leaf_kv, first_row, LEAF_DEV, 0).reshape(LEAF_DEV, KVH, 2, HD).astype(jnp.float32)
        segment = lax.dynamic_index_in_dim(leaf_seg, block_index, 0, keepdims=False)
        own_leaf = lax.dynamic_index_in_dim(leaf_block, block_index, 0, keepdims=False).astype(jnp.int32)
        reach_row = lax.dynamic_index_in_dim(ancestors, own_leaf, 0, keepdims=False) > 0.5
        doc_visible = jnp.repeat(reach_row, DOC_DEV)
        leaf_visible = (segment[:, None] == segment[None, :]) & (positions[None, :] <= positions[:, None])
        visible = jnp.concatenate([jnp.broadcast_to(doc_visible[None, :], (LEAF_DEV, DOC)), leaf_visible], axis=1)
        key_rows = jnp.concatenate([doc_keys, leaf_pairs[:, :, 0]], axis=0)
        value_rows = jnp.concatenate([doc_values, leaf_pairs[:, :, 1]], axis=0)
        logits = jnp.einsum('ikgd,jkd->kgij', queries, key_rows) * score_scale
        logits = jnp.where(visible[None, None], logits, -jnp.inf)
        row_max = jnp.max(logits, axis=-1, keepdims=True)
        exponent = jnp.exp(logits - row_max)
        probability = exponent / jnp.sum(exponent, axis=-1, keepdims=True)
        rounded = held_bf16(probability)
        output = jnp.einsum('kgij,jkd->ikgd', rounded, value_rows)
        grad_dot = jnp.transpose(jnp.sum(out_grads * output, axis=-1), (1, 2, 0))
        grad_prob = jnp.einsum('ikgd,jkd->kgij', out_grads, value_rows)
        grad_logit = held_bf16(probability * (grad_prob - grad_dot[..., None]))
        query_grad = (score_scale * jnp.einsum('kgij,jkd->ikgd', grad_logit, key_rows)).astype(jnp.bfloat16)
        grad_key = score_scale * jnp.einsum('kgij,ikgd->jkd', grad_logit, queries)
        grad_value = jnp.einsum('kgij,ikgd->jkd', rounded, out_grads)
        grad_pairs = jnp.stack([grad_key, grad_value], axis=2)
        leaf_grads = grad_pairs[DOC:].astype(jnp.bfloat16).reshape(LEAF_DEV, KVH * 2 * HD)
        return running + grad_pairs[:DOC], (query_grad.reshape(LEAF_DEV, QH * HD), leaf_grads)

    start_sum = jnp.zeros((DOC, KVH, 2, HD), jnp.float32)
    doc_sum, outputs = lax.scan(one_block, start_sum, jnp.arange(NBLK, dtype=jnp.int32))
    query_grad = outputs[0].reshape(QTOK, QH * HD)
    leaf_kv_grad = outputs[1].reshape(QTOK, KVH * 2 * HD)
    doc_kv_grad = doc_sum.reshape(DOC, KVH * 2 * HD).astype(jnp.bfloat16)
    return (query_grad, leaf_kv_grad, doc_kv_grad)
```

```python
import functools

import jax
import jax.numpy as jnp
from jax import lax
from jax.experimental import pallas as pl
from jax.experimental.pallas import tpu as pltpu
from jax.sharding import PartitionSpec as P

QH = 40
KVH = 8
HD = 128
GROUPS = QH // KVH
SCALE = HD ** (-0.5)
LOG2E = 1.4426950408889634
HIDDEN = -1e30
NN = (((1,), (0,)), ((), ()))
NT = (((1,), (1,)), ((), ()))
TN = (((0,), (0,)), ((), ()))


def hop_orders(tok_size):
    bits = [1 << b for b in range(tok_size.bit_length() - 1)]
    far = bits[:0:-1]
    other = far if len(far) < 3 else far[:-2] + [far[-1], far[-2]]
    return far, other


def dot(a, b, dims):
    return lax.dot_general(a, b, dims, preferred_element_type=jnp.float32)


def attention_kernel(
    tok_size,
    orders,
    parent,
    leaf_block,
    q_ref,
    go_ref,
    leaf_ref,
    near_ref,
    far_ref,
    bias_ref,
    dq_ref,
    dleaf_ref,
    dnear_ref,
    dfar_ref,
    seen,
    place,
    count,
    keys,
    prob,
    dlog,
    grads,
):
    leaf_rows = leaf_ref.shape[0]
    doc_rows = near_ref.shape[0] + far_ref.shape[0]
    half = tok_size // 2
    block = doc_rows // tok_size

    @pl.when(pl.program_id(0) == 0)
    def find_visible():
        keys[...] = jnp.zeros_like(keys)
        me = lax.axis_index("tok")
        core = lax.rem(me, 2)

        def clear(i, carry):
            seen[i] = 0
            return carry

        lax.fori_loop(0, tok_size, clear, 0)

        def climb(i, node):
            seen[node] = 1
            return parent[node]

        lax.fori_loop(0, tok_size, climb, leaf_block[me])
        filled = jnp.int32(0)
        for position in range(tok_size):
            local = position % half
            same = sum(m for r, m in enumerate(orders[0]) if local >> r & 1)
            cross = sum(m for r, m in enumerate(orders[1]) if local >> r & 1)
            if position < half:
                owner = me ^ jnp.where(core == 0, same, cross)
            else:
                owner = me ^ 1 ^ jnp.where(core == 0, cross, same)
            visible = seen[owner]
            place[position] = jnp.where(visible == 1, filled, -1)
            filled = filled + visible
        count[0] = filled

    total = count[0]

    def each_block(act):
        for position in range(tok_size):
            act(position, place[position])

    def load_block(position, slot):
        source = near_ref if position < half else far_ref
        first = (position % half) * block

        @pl.when(slot >= 0)
        def _():
            row = pl.multiple_of(leaf_rows + slot * block, block)
            keys[pl.ds(row, block), :] = source[first : first + block, :]

    each_block(load_block)
    keys[:leaf_rows, :] = leaf_ref[...]

    def process(doc_len):
        length = leaf_rows + doc_len
        all_keys = keys[:length, :HD]
        all_values = keys[:length, HD:]
        row = lax.broadcasted_iota(jnp.int32, (doc_len, 1), 0)
        doc_live = row < total * block
        for r in range(GROUPS):
            cols = slice(r * HD, (r + 1) * HD)
            rows = slice(r * leaf_rows, (r + 1) * leaf_rows)
            q = q_ref[:, cols]
            go = go_ref[:, cols]
            logit = dot(all_keys, q, NT)
            leaf_logit = logit[:leaf_rows] + bias_ref[...]
            doc_logit = jnp.where(doc_live, logit[leaf_rows:], HIDDEN)
            logit = jnp.concatenate([leaf_logit, doc_logit], axis=0)
            top = jnp.max(logit, axis=0, keepdims=True)
            weight = jnp.exp2((logit - top) * (SCALE * LOG2E))
            inverse = 1.0 / jnp.sum(weight, axis=0, keepdims=True)
            grad_prob = dot(all_values, go, NT)
            probability = weight * inverse
            grad_dot = jnp.sum(probability * grad_prob, axis=0, keepdims=True)
            prob[:length, rows] = probability.astype(jnp.bfloat16)
            grad_logit = (probability * (grad_prob - grad_dot)).astype(jnp.bfloat16)
            dlog[:length, rows] = grad_logit
            dq = dot(all_keys, grad_logit, TN) * SCALE
            dq_ref[:, cols] = jnp.transpose(dq).astype(jnp.bfloat16)
        q_all = jnp.concatenate([q_ref[:, r * HD : (r + 1) * HD] for r in range(GROUPS)], axis=0)
        go_all = jnp.concatenate([go_ref[:, r * HD : (r + 1) * HD] for r in range(GROUPS)], axis=0)
        grads[:length, :HD] = dot(dlog[:length, :], q_all, NN) * SCALE
        grads[:length, HD:] = dot(prob[:length, :], go_all, NN)

    lengths = [doc_rows // 4 * k for k in (1, 2, 3, 4)]
    for i, doc_len in enumerate(lengths):
        low = 0 if i == 0 else lengths[i - 1] // block

        @pl.when((total > low) & (total <= doc_len // block))
        def _(doc_len=doc_len):
            process(doc_len)

    dleaf_ref[...] = grads[:leaf_rows, :].astype(jnp.bfloat16)

    def store_block(position, slot):
        target = dnear_ref if position < half else dfar_ref
        first = (position % half) * block

        @pl.when(slot >= 0)
        def _():
            row = pl.multiple_of(leaf_rows + slot * block, block)
            target[first : first + block, :] = grads[pl.ds(row, block), :].astype(target.dtype)

        @pl.when(slot < 0)
        def _():
            target[first : first + block, :] = jnp.zeros((block, 2 * HD), target.dtype)

    each_block(store_block)


def attention(tok_size, orders, query, leaf_kv, near, far, grad_out, bias, block_parent, leaf_block):
    rows = query.shape[0]
    local_heads = leaf_kv.shape[1] // (2 * HD)
    half_rows = near.shape[0]
    length = rows + 2 * half_rows
    wide = pl.BlockSpec((rows, GROUPS * HD), lambda g, *_: (0, g))
    pair = pl.BlockSpec((rows, 2 * HD), lambda g, *_: (0, g))
    docs = pl.BlockSpec((half_rows, 2 * HD), lambda g, *_: (0, g))
    return pl.pallas_call(
        functools.partial(attention_kernel, tok_size, orders),
        out_shape=(
            jax.ShapeDtypeStruct(query.shape, jnp.bfloat16),
            jax.ShapeDtypeStruct(leaf_kv.shape, jnp.bfloat16),
            jax.ShapeDtypeStruct(near.shape, jnp.float32),
            jax.ShapeDtypeStruct(far.shape, jnp.bfloat16),
        ),
        grid_spec=pltpu.PrefetchScalarGridSpec(
            num_scalar_prefetch=2,
            grid=(local_heads,),
            in_specs=[
                wide,
                wide,
                pair,
                docs,
                docs,
                pl.BlockSpec((rows, rows), lambda g, *_: (0, 0)),
            ],
            out_specs=[wide, pair, docs, docs],
            scratch_shapes=[
                pltpu.SMEM((tok_size,), jnp.int32),
                pltpu.SMEM((tok_size,), jnp.int32),
                pltpu.SMEM((1,), jnp.int32),
                pltpu.VMEM((length, 2 * HD), jnp.bfloat16),
                pltpu.VMEM((length, GROUPS * rows), jnp.bfloat16),
                pltpu.VMEM((length, GROUPS * rows), jnp.bfloat16),
                pltpu.VMEM((length, 2 * HD), jnp.float32),
            ],
        ),
        compiler_params=pltpu.CompilerParams(vmem_limit_bytes=56 * 1024 * 1024),
        name="tree_attention_backward",
    )(block_parent, leaf_block, query, grad_out, leaf_kv, near, far, bias)


def body(tok_size, head_size, query, leaf_kv, doc_kv, grad_out, block_parent, leaf_block, leaf_seg):
    rows = query.shape[0]
    width = leaf_kv.shape[1]
    orders = hop_orders(tok_size)
    head = lax.axis_index("head")
    swap_head = [(0, 1), (1, 0)]

    def exchange(value, round_index):
        pairs = [(i, i ^ orders[i % 2][round_index]) for i in range(tok_size)]
        return lax.ppermute(value, "tok", pairs)

    def swap_core(value):
        return lax.ppermute(value, "tok", [(i, i ^ 1) for i in range(tok_size)])

    if head_size == 2:
        own = lax.dynamic_slice_in_dim(doc_kv, head * width, width, 1)
        other = lax.dynamic_slice_in_dim(doc_kv, (1 - head) * width, width, 1)
        held = jnp.concatenate([own, lax.ppermute(other, "head", swap_head)], axis=0)
    else:
        held = lax.all_to_all(doc_kv, "head", split_axis=1, concat_axis=0, tiled=True)
    rounds = len(orders[0])
    for r in range(rounds):
        held = jnp.concatenate([held, exchange(held, r)], axis=0)
    crossed = swap_core(held)

    segment = leaf_seg[0]
    positions = jnp.arange(rows, dtype=jnp.int32)
    allowed = (segment[:, None] == segment[None, :]) & (positions[:, None] <= positions[None, :])
    bias = jnp.where(allowed, 0.0, HIDDEN).astype(jnp.float32)

    query_grad, leaf_grad, total, sent = attention(
        tok_size, orders, query, leaf_kv, held, crossed, grad_out, bias, block_parent, leaf_block
    )
    total = total + swap_core(sent).astype(jnp.float32)
    for r in reversed(range(rounds)):
        kept = total.shape[0] // 2
        arrived = exchange(total[kept:].astype(jnp.bfloat16), r)
        total = total[:kept] + arrived.astype(jnp.float32)
    total = total.astype(jnp.bfloat16)
    if head_size == 2:
        kept = total.shape[0] // 2
        mine = total[:kept]
        arrived = lax.ppermute(total[kept:], "head", swap_head)
        doc_grad = jnp.where(
            head == 0,
            jnp.concatenate([mine, arrived], axis=1),
            jnp.concatenate([arrived, mine], axis=1),
        )
    else:
        doc_grad = lax.all_to_all(total, "head", split_axis=0, concat_axis=1, tiled=True)
    return query_grad, leaf_grad, doc_grad


def solution(mesh):
    placed = (
        P("tok", "head"),
        P("tok", "head"),
        P(("tok", "head"), None),
        P("tok", "head"),
        P(),
        P(),
        P("tok", None),
    )
    return jax.shard_map(
        functools.partial(body, mesh.shape["tok"], mesh.shape["head"]),
        mesh=mesh,
        in_specs=placed,
        out_specs=(P("tok", "head"), P("tok", "head"), P(("tok", "head"), None)),
        check_vma=False,
    )
```

```python
import functools

import jax
import jax.numpy as jnp
from jax import lax
from jax.experimental import pallas as pl
from jax.experimental.pallas import tpu as pltpu
from jax.sharding import PartitionSpec as P

QH = 40
KVH = 8
HD = 128
GROUPS = QH // KVH
SCALE = HD ** (-0.5)
LOG2E = 1.4426950408889634
HIDDEN = -1e30
NN = (((1,), (0,)), ((), ()))
NT = (((1,), (1,)), ((), ()))
TN = (((0,), (0,)), ((), ()))


def hop_orders(tok_size):
    bits = [1 << b for b in range(tok_size.bit_length() - 1)]
    far = bits[:0:-1]
    other = far if len(far) < 3 else far[:-2] + [far[-1], far[-2]]
    return far, other


def dot(a, b, dims):
    return lax.dot_general(a, b, dims, preferred_element_type=jnp.float32)


def weights(logit, top):
    return jnp.exp2((logit - top) * (SCALE * LOG2E))


def lanes(h, width, first, size):
    return pl.ds(pl.multiple_of(h * width + first, HD), size)


def leaf_kernel(seg_ref, q_ref, go_ref, leaf_ref, stats_ref, bias_ref):
    rows = leaf_ref.shape[0]
    heads = stats_ref.shape[0]
    across = jnp.broadcast_to(seg_ref[...].astype(jnp.float32), (rows, rows))
    down = jnp.transpose(across)
    key = lax.broadcasted_iota(jnp.int32, (rows, rows), 0)
    asker = lax.broadcasted_iota(jnp.int32, (rows, rows), 1)
    bias_ref[...] = jnp.where((across == down) & (key <= asker), 0.0, HIDDEN)

    def one_head(h, carry):
        leaf_keys = leaf_ref[:, lanes(h, 2 * HD, 0, HD)]
        leaf_values = leaf_ref[:, lanes(h, 2 * HD, HD, HD)]
        for r in range(GROUPS):
            cols = lanes(h, GROUPS * HD, r * HD, HD)
            logit = dot(leaf_keys, q_ref[:, cols], NT) + bias_ref[...]
            top = jnp.max(logit, axis=0, keepdims=True)
            weight = weights(logit, top)
            grad_prob = dot(leaf_values, go_ref[:, cols], NT)
            stats_ref[h, 0, r : r + 1, :] = top
            stats_ref[h, 1, r : r + 1, :] = jnp.sum(weight, axis=0, keepdims=True)
            stats_ref[h, 2, r : r + 1, :] = jnp.sum(weight * grad_prob, axis=0, keepdims=True)
        return carry

    lax.fori_loop(0, heads, one_head, 0)


def doc_kernel(
    tok_size,
    orders,
    parent,
    leaf_block,
    q_ref,
    go_ref,
    near_ref,
    far_ref,
    stats_ref,
    dnear_ref,
    dfar_ref,
    final_ref,
    keys_ref,
    dlog_ref,
    count_ref,
    seen,
    place,
    prob,
    grads,
):
    rows = q_ref.shape[0]
    heads = stats_ref.shape[0]
    doc_rows = near_ref.shape[0] + far_ref.shape[0]
    half = tok_size // 2
    block = doc_rows // tok_size
    keys_ref[...] = jnp.zeros_like(keys_ref)
    me = lax.axis_index("tok")
    core = lax.rem(me, 2)

    def clear(i, carry):
        seen[i] = 0
        return carry

    lax.fori_loop(0, tok_size, clear, 0)

    def climb(i, node):
        seen[node] = 1
        return parent[node]

    lax.fori_loop(0, tok_size, climb, leaf_block[me])
    total = jnp.int32(0)
    for position in range(tok_size):
        local = position % half
        same = sum(m for r, m in enumerate(orders[0]) if local >> r & 1)
        cross = sum(m for r, m in enumerate(orders[1]) if local >> r & 1)
        if position < half:
            owner = me ^ jnp.where(core == 0, same, cross)
        else:
            owner = me ^ 1 ^ jnp.where(core == 0, cross, same)
        visible = seen[owner]
        place[position] = jnp.where(visible == 1, total, -1)
        total = total + visible
    count_ref[0] = total

    for position in range(tok_size):
        source = near_ref if position < half else far_ref
        first = (position % half) * block
        slot = place[position]

        @pl.when(slot >= 0)
        def _(source=source, first=first, slot=slot):
            row = pl.multiple_of(slot * block, block)
            keys_ref[pl.ds(row, block), :] = source[first : first + block, :]

    def process(length):
        live = lax.broadcasted_iota(jnp.int32, (length, 1), 0) < total * block

        def one_head(h, carry):
            doc_keys = keys_ref[:length, lanes(h, 2 * HD, 0, HD)]
            doc_values = keys_ref[:length, lanes(h, 2 * HD, HD, HD)]
            for r in range(GROUPS):
                cols = lanes(h, GROUPS * HD, r * HD, HD)
                logit = jnp.where(live, dot(doc_keys, q_ref[:, cols], NT), HIDDEN)
                leaf_top = stats_ref[h, 0, r : r + 1, :]
                top = jnp.maximum(leaf_top, jnp.max(logit, axis=0, keepdims=True))
                shrink = weights(leaf_top, top)
                weight = weights(logit, top)
                leaf_sum = stats_ref[h, 1, r : r + 1, :] * shrink
                leaf_dot = stats_ref[h, 2, r : r + 1, :] * shrink
                inverse = 1.0 / (leaf_sum + jnp.sum(weight, axis=0, keepdims=True))
                grad_prob = dot(doc_values, go_ref[:, cols], NT)
                grad_dot = leaf_dot + jnp.sum(weight * grad_prob, axis=0, keepdims=True)
                grad_dot = grad_dot * inverse
                probability = weight * inverse
                prob[:length, r * rows : (r + 1) * rows] = probability.astype(jnp.bfloat16)
                grad_logit = (probability * (grad_prob - grad_dot)).astype(jnp.bfloat16)
                dlog_ref[h, :length, r * rows : (r + 1) * rows] = grad_logit
                final_ref[h, 0, r : r + 1, :] = top
                final_ref[h, 1, r : r + 1, :] = inverse
                final_ref[h, 2, r : r + 1, :] = grad_dot
            q_all = stacked(q_ref, h)
            go_all = stacked(go_ref, h)
            grad_key = dot(dlog_ref[h, :length, :], q_all, NN) * SCALE
            grads[:length, lanes(h, 2 * HD, 0, HD)] = grad_key
            grads[:length, lanes(h, 2 * HD, HD, HD)] = dot(prob[:length, :], go_all, NN)
            return carry

        lax.fori_loop(0, heads, one_head, 0)

    for_each_length(total, doc_rows, block, process)

    for position in range(tok_size):
        target = dnear_ref if position < half else dfar_ref
        first = (position % half) * block
        slot = place[position]

        @pl.when(slot >= 0)
        def _(target=target, first=first, slot=slot):
            row = pl.multiple_of(slot * block, block)
            target[first : first + block, :] = grads[pl.ds(row, block), :].astype(target.dtype)

        @pl.when(slot < 0)
        def _(target=target, first=first):
            target[first : first + block, :] = jnp.zeros((block, target.shape[1]), target.dtype)


def stacked(ref, h):
    return jnp.concatenate([ref[:, lanes(h, GROUPS * HD, r * HD, HD)] for r in range(GROUPS)], axis=0)


def for_each_length(total, doc_rows, block, process):
    lengths = [doc_rows // 4 * k for k in (1, 2, 3, 4)]
    for i, length in enumerate(lengths):
        low = 0 if i == 0 else lengths[i - 1] // block

        @pl.when((total > low) & (total <= length // block))
        def _(length=length):
            process(length)


def query_kernel(
    block,
    count_ref,
    q_ref,
    go_ref,
    leaf_ref,
    bias_ref,
    final_ref,
    keys_ref,
    dlog_ref,
    dq_ref,
    dleaf_ref,
    prob,
    dlog,
):
    h = pl.program_id(0)
    rows = q_ref.shape[0]
    total = count_ref[0]
    leaf_keys = leaf_ref[:, :HD]
    leaf_values = leaf_ref[:, HD:]
    leaf_turned = jnp.transpose(leaf_keys)
    for r in range(GROUPS):
        cols = slice(r * HD, (r + 1) * HD)
        logit = dot(leaf_keys, q_ref[:, cols], NT) + bias_ref[...]
        probability = weights(logit, final_ref[h, 0, r : r + 1, :]) * final_ref[h, 1, r : r + 1, :]
        grad_prob = dot(leaf_values, go_ref[:, cols], NT)
        grad_logit = probability * (grad_prob - final_ref[h, 2, r : r + 1, :])
        prob[:, r * rows : (r + 1) * rows] = probability.astype(jnp.bfloat16)
        dlog[:, r * rows : (r + 1) * rows] = grad_logit.astype(jnp.bfloat16)
    q_all = jnp.concatenate([q_ref[:, r * HD : (r + 1) * HD] for r in range(GROUPS)], axis=0)
    go_all = jnp.concatenate([go_ref[:, r * HD : (r + 1) * HD] for r in range(GROUPS)], axis=0)
    grad_key = dot(dlog[...], q_all, NN) * SCALE
    dleaf_ref[:, :HD] = grad_key.astype(jnp.bfloat16)
    dleaf_ref[:, HD:] = dot(prob[...], go_all, NN).astype(jnp.bfloat16)

    def process(length):
        doc_turned = jnp.transpose(keys_ref[:length, lanes(h, 2 * HD, 0, HD)])
        for r in range(GROUPS):
            part = slice(r * rows, (r + 1) * rows)
            dq = dot(leaf_turned, dlog[:, part], NN)
            dq = dq + dot(doc_turned, dlog_ref[h, :length, part], NN)
            dq_ref[:, r * HD : (r + 1) * HD] = jnp.transpose(dq * SCALE).astype(jnp.bfloat16)

    for_each_length(total, keys_ref.shape[0], block, process)


IN_VMEM = pl.BlockSpec(memory_space=pltpu.VMEM)
IN_SMEM = pl.BlockSpec(memory_space=pltpu.SMEM)
PARAMS = pltpu.CompilerParams(vmem_limit_bytes=40 * 1024 * 1024)


def shape(dims, dtype):
    return jax.ShapeDtypeStruct(dims, dtype)


def cost(queries, pairs, matmuls, extra):
    return pl.CostEstimate(
        flops=2 * HD * pairs * queries * matmuls,
        bytes_accessed=4 * HD * queries + extra,
        transcendentals=pairs * queries,
    )


def leaf_stats(leaf_seg, query, grad_out, leaf_kv):
    rows = query.shape[0]
    heads = leaf_kv.shape[1] // (2 * HD)
    return pl.pallas_call(
        leaf_kernel,
        out_shape=(shape((heads, 3, 8, rows), jnp.float32), shape((rows, rows), jnp.float32)),
        in_specs=[IN_VMEM] * 4,
        out_specs=(IN_VMEM,) * 2,
        compiler_params=PARAMS,
        cost_estimate=cost(rows * heads * GROUPS, rows, 4, 0),
        name="leaf_stats",
    )(leaf_seg, query, grad_out, leaf_kv)


def doc_grads(tok_size, orders, block_parent, leaf_block, query, grad_out, near, far, stats):
    rows = query.shape[0]
    heads = stats.shape[0]
    doc_rows = 2 * near.shape[0]
    return pl.pallas_call(
        functools.partial(doc_kernel, tok_size, orders),
        out_shape=(
            shape(near.shape, jnp.float32),
            shape(far.shape, jnp.bfloat16),
            shape(stats.shape, jnp.float32),
            shape((doc_rows, near.shape[1]), jnp.bfloat16),
            shape((heads, doc_rows, GROUPS * rows), jnp.bfloat16),
            shape((1,), jnp.int32),
        ),
        in_specs=[IN_SMEM] * 2 + [IN_VMEM] * 5,
        out_specs=(IN_VMEM,) * 5 + (IN_SMEM,),
        scratch_shapes=[
            pltpu.SMEM((tok_size,), jnp.int32),
            pltpu.SMEM((tok_size,), jnp.int32),
            pltpu.VMEM((doc_rows, GROUPS * rows), jnp.bfloat16),
            pltpu.VMEM((doc_rows, near.shape[1]), jnp.float32),
        ],
        compiler_params=PARAMS,
        cost_estimate=cost(rows * heads * GROUPS, doc_rows, 4, 0),
        name="doc_grads",
    )(block_parent, leaf_block, query, grad_out, near, far, stats)


def query_grads(block, count, query, grad_out, leaf_kv, bias, final, keys, dlog):
    rows = query.shape[0]
    heads = final.shape[0]
    wide = pl.BlockSpec((rows, GROUPS * HD), lambda g: (0, g))
    pair = pl.BlockSpec((rows, 2 * HD), lambda g: (0, g))
    return pl.pallas_call(
        functools.partial(query_kernel, block),
        out_shape=(shape(query.shape, jnp.bfloat16), shape(leaf_kv.shape, jnp.bfloat16)),
        grid=(heads,),
        in_specs=[IN_SMEM, wide, wide, pair, IN_VMEM, IN_VMEM, IN_VMEM, IN_VMEM],
        out_specs=(wide, pair),
        scratch_shapes=[pltpu.VMEM((rows, GROUPS * rows), jnp.bfloat16)] * 2,
        compiler_params=PARAMS,
        cost_estimate=cost(rows * heads * GROUPS, rows, 8, 0),
        name="query_grads",
    )(count, query, grad_out, leaf_kv, bias, final, keys, dlog)


def body(tok_size, head_size, query, leaf_kv, doc_kv, grad_out, block_parent, leaf_block, leaf_seg):
    width = leaf_kv.shape[1]
    orders = hop_orders(tok_size)
    head = lax.axis_index("head")
    swap_head = [(0, 1), (1, 0)]

    def exchange(value, round_index):
        pairs = [(i, i ^ orders[i % 2][round_index]) for i in range(tok_size)]
        return lax.ppermute(value, "tok", pairs)

    def swap_core(value):
        return lax.ppermute(value, "tok", [(i, i ^ 1) for i in range(tok_size)])

    if head_size == 2:
        own = lax.dynamic_slice_in_dim(doc_kv, head * width, width, 1)
        other = lax.dynamic_slice_in_dim(doc_kv, (1 - head) * width, width, 1)
        held = jnp.concatenate([own, lax.ppermute(other, "head", swap_head)], axis=0)
    else:
        held = lax.all_to_all(doc_kv, "head", split_axis=1, concat_axis=0, tiled=True)
    rounds = len(orders[0])
    for r in range(rounds):
        if r == rounds - 1:
            held, leaf_kv = lax.optimization_barrier((held, leaf_kv))
        held = jnp.concatenate([held, exchange(held, r)], axis=0)
    crossed = swap_core(held)
    near_rows = held.shape[0]

    stats, bias = leaf_stats(leaf_seg, query, grad_out, leaf_kv)
    total, sent, final, keys, dlog, count = doc_grads(
        tok_size, orders, block_parent, leaf_block, query, grad_out, held, crossed, stats
    )
    total = total + swap_core(sent).astype(jnp.float32)
    for r in reversed(range(rounds)):
        kept = total.shape[0] // 2
        leaving = total[kept:].astype(jnp.bfloat16)
        if r == rounds - 1:
            leaving, final = lax.optimization_barrier((leaving, final))
        arrived = exchange(leaving, r)
        total = total[:kept] + arrived.astype(jnp.float32)
    block = 2 * near_rows // tok_size
    query_grad, leaf_grad = query_grads(block, count, query, grad_out, leaf_kv, bias, final, keys, dlog)
    total = total.astype(jnp.bfloat16)
    if head_size == 2:
        kept = total.shape[0] // 2
        mine = total[:kept]
        arrived = lax.ppermute(total[kept:], "head", swap_head)
        doc_grad = jnp.where(
            head == 0,
            jnp.concatenate([mine, arrived], axis=1),
            jnp.concatenate([arrived, mine], axis=1),
        )
    else:
        doc_grad = lax.all_to_all(total, "head", split_axis=0, concat_axis=1, tiled=True)
    return query_grad, leaf_grad, doc_grad


def solution(mesh):
    placed = (
        P("tok", "head"),
        P("tok", "head"),
        P(("tok", "head"), None),
        P("tok", "head"),
        P(),
        P(),
        P("tok", None),
    )
    return jax.shard_map(
        functools.partial(body, mesh.shape["tok"], mesh.shape["head"]),
        mesh=mesh,
        in_specs=placed,
        out_specs=(P("tok", "head"), P("tok", "head"), P(("tok", "head"), None)),
        check_vma=False,
    )
```

```python
import functools

import jax
import jax.numpy as jnp
from jax import lax
from jax.experimental import pallas as pl
from jax.experimental.pallas import tpu as pltpu
from jax.sharding import PartitionSpec as P

QH = 40
KVH = 8
HD = 128
GROUPS = QH // KVH
SCALE = HD ** (-0.5)
LOG2E = 1.4426950408889634
HIDDEN = -1e30
NN = (((1,), (0,)), ((), ()))
NT = (((1,), (1,)), ((), ()))
TN = (((0,), (0,)), ((), ()))


def hop_orders(tok_size):
    bits = [1 << b for b in range(tok_size.bit_length() - 1)]
    far = bits[:0:-1]
    other = far if len(far) < 3 else far[:-2] + [far[-1], far[-2]]
    return far, other


def dot(a, b, dims):
    return lax.dot_general(a, b, dims, preferred_element_type=jnp.float32)


def weights(logit, top):
    return jnp.exp2((logit - top) * (SCALE * LOG2E))


def lanes(h, width, first, size):
    return pl.ds(pl.multiple_of(h * width + first, HD), size)


def leaf_kernel(seg_ref, q_ref, go_ref, leaf_ref, stats_ref, bias_ref):
    rows = leaf_ref.shape[0]
    heads = stats_ref.shape[0]
    across = jnp.broadcast_to(seg_ref[...].astype(jnp.float32), (rows, rows))
    down = jnp.transpose(across)
    key = lax.broadcasted_iota(jnp.int32, (rows, rows), 0)
    asker = lax.broadcasted_iota(jnp.int32, (rows, rows), 1)
    bias_ref[...] = jnp.where((across == down) & (key <= asker), 0.0, HIDDEN)

    def one_head(h, carry):
        leaf_keys = leaf_ref[:, lanes(h, 2 * HD, 0, HD)]
        leaf_values = leaf_ref[:, lanes(h, 2 * HD, HD, HD)]
        for r in range(GROUPS):
            cols = lanes(h, GROUPS * HD, r * HD, HD)
            logit = dot(leaf_keys, q_ref[:, cols], NT) + bias_ref[...]
            top = jnp.max(logit, axis=0, keepdims=True)
            weight = weights(logit, top)
            grad_prob = dot(leaf_values, go_ref[:, cols], NT)
            stats_ref[h, 0, r : r + 1, :] = top
            stats_ref[h, 1, r : r + 1, :] = jnp.sum(weight, axis=0, keepdims=True)
            stats_ref[h, 2, r : r + 1, :] = jnp.sum(weight * grad_prob, axis=0, keepdims=True)
        return carry

    lax.fori_loop(0, heads, one_head, 0)


def doc_kernel(
    tok_size,
    orders,
    parent,
    leaf_block,
    q_ref,
    go_ref,
    near_ref,
    far_ref,
    stats_ref,
    dnear_ref,
    dfar_ref,
    final_ref,
    keys_ref,
    dlog_ref,
    count_ref,
    seen,
    place,
    prob,
    grads,
):
    rows = q_ref.shape[0]
    heads = stats_ref.shape[0]
    doc_rows = near_ref.shape[0] + far_ref.shape[0]
    half = tok_size // 2
    block = doc_rows // tok_size
    keys_ref[...] = jnp.zeros_like(keys_ref)
    me = lax.axis_index("tok")
    core = lax.rem(me, 2)

    def clear(i, carry):
        seen[i] = 0
        return carry

    lax.fori_loop(0, tok_size, clear, 0)

    def climb(i, node):
        seen[node] = 1
        return parent[node]

    lax.fori_loop(0, tok_size, climb, leaf_block[me])
    total = jnp.int32(0)
    for position in range(tok_size):
        local = position % half
        same = sum(m for r, m in enumerate(orders[0]) if local >> r & 1)
        cross = sum(m for r, m in enumerate(orders[1]) if local >> r & 1)
        if position < half:
            owner = me ^ jnp.where(core == 0, same, cross)
        else:
            owner = me ^ 1 ^ jnp.where(core == 0, cross, same)
        visible = seen[owner]
        place[position] = jnp.where(visible == 1, total, -1)
        total = total + visible
    count_ref[0] = total * block

    for position in range(tok_size):
        source = near_ref if position < half else far_ref
        first = (position % half) * block
        slot = place[position]

        @pl.when(slot >= 0)
        def _(source=source, first=first, slot=slot):
            row = pl.multiple_of(slot * block, block)
            keys_ref[pl.ds(row, block), :] = source[first : first + block, :]

    def process(length):
        live = lax.broadcasted_iota(jnp.int32, (length, 1), 0) < total * block

        def one_head(h, carry):
            doc_keys = keys_ref[:length, lanes(h, 2 * HD, 0, HD)]
            doc_values = keys_ref[:length, lanes(h, 2 * HD, HD, HD)]
            for r in range(GROUPS):
                cols = lanes(h, GROUPS * HD, r * HD, HD)
                logit = jnp.where(live, dot(doc_keys, q_ref[:, cols], NT), HIDDEN)
                leaf_top = stats_ref[h, 0, r : r + 1, :]
                top = jnp.maximum(leaf_top, jnp.max(logit, axis=0, keepdims=True))
                shrink = weights(leaf_top, top)
                weight = weights(logit, top)
                leaf_sum = stats_ref[h, 1, r : r + 1, :] * shrink
                leaf_dot = stats_ref[h, 2, r : r + 1, :] * shrink
                inverse = 1.0 / (leaf_sum + jnp.sum(weight, axis=0, keepdims=True))
                grad_prob = dot(doc_values, go_ref[:, cols], NT)
                grad_dot = leaf_dot + jnp.sum(weight * grad_prob, axis=0, keepdims=True)
                grad_dot = grad_dot * inverse
                probability = weight * inverse
                prob[:length, r * rows : (r + 1) * rows] = probability.astype(jnp.bfloat16)
                grad_logit = (probability * (grad_prob - grad_dot)).astype(jnp.bfloat16)
                dlog_ref[h, :length, r * rows : (r + 1) * rows] = grad_logit
                final_ref[h, 0, r : r + 1, :] = top
                final_ref[h, 1, r : r + 1, :] = inverse
                final_ref[h, 2, r : r + 1, :] = grad_dot
            q_all = stacked(q_ref, h)
            go_all = stacked(go_ref, h)
            grad_key = dot(dlog_ref[h, :length, :], q_all, NN) * SCALE
            grads[:length, lanes(h, 2 * HD, 0, HD)] = grad_key
            grads[:length, lanes(h, 2 * HD, HD, HD)] = dot(prob[:length, :], go_all, NN)
            return carry

        lax.fori_loop(0, heads, one_head, 0)

    for_each_length(total * block, doc_rows, process)

    for position in range(tok_size):
        target = dnear_ref if position < half else dfar_ref
        first = (position % half) * block
        slot = place[position]

        @pl.when(slot >= 0)
        def _(target=target, first=first, slot=slot):
            row = pl.multiple_of(slot * block, block)
            target[first : first + block, :] = grads[pl.ds(row, block), :].astype(target.dtype)

        @pl.when(slot < 0)
        def _(target=target, first=first):
            target[first : first + block, :] = jnp.zeros((block, target.shape[1]), target.dtype)


def stacked(ref, h):
    return jnp.concatenate([ref[:, lanes(h, GROUPS * HD, r * HD, HD)] for r in range(GROUPS)], axis=0)


def for_each_length(live_rows, doc_rows, process):
    lengths = [doc_rows // 4 * k for k in (1, 2, 3, 4)]
    for low, length in zip([0] + lengths, lengths):

        @pl.when((live_rows > low) & (live_rows <= length))
        def _(length=length):
            process(length)


def query_kernel(
    first_head,
    n_done,
    count_ref,
    q_ref,
    go_ref,
    leaf_ref,
    bias_ref,
    final_ref,
    keys_ref,
    dlog_ref,
    *rest,
):
    dq_ref, dleaf_ref, prob, dlog = rest[n_done:]
    h = first_head + pl.program_id(0)
    rows = q_ref.shape[0]
    leaf_keys = leaf_ref[:, :HD]
    leaf_values = leaf_ref[:, HD:]
    leaf_turned = jnp.transpose(leaf_keys)
    for r in range(GROUPS):
        cols = slice(r * HD, (r + 1) * HD)
        logit = dot(leaf_keys, q_ref[:, cols], NT) + bias_ref[...]
        probability = weights(logit, final_ref[h, 0, r : r + 1, :]) * final_ref[h, 1, r : r + 1, :]
        grad_prob = dot(leaf_values, go_ref[:, cols], NT)
        grad_logit = probability * (grad_prob - final_ref[h, 2, r : r + 1, :])
        prob[:, r * rows : (r + 1) * rows] = probability.astype(jnp.bfloat16)
        dlog[:, r * rows : (r + 1) * rows] = grad_logit.astype(jnp.bfloat16)
    q_all = jnp.concatenate([q_ref[:, r * HD : (r + 1) * HD] for r in range(GROUPS)], axis=0)
    go_all = jnp.concatenate([go_ref[:, r * HD : (r + 1) * HD] for r in range(GROUPS)], axis=0)
    grad_key = dot(dlog[...], q_all, NN) * SCALE
    dleaf_ref[:, :HD] = grad_key.astype(jnp.bfloat16)
    dleaf_ref[:, HD:] = dot(prob[...], go_all, NN).astype(jnp.bfloat16)

    def process(length):
        doc_turned = jnp.transpose(keys_ref[:length, lanes(h, 2 * HD, 0, HD)])
        for r in range(GROUPS):
            part = slice(r * rows, (r + 1) * rows)
            dq = dot(leaf_turned, dlog[:, part], NN)
            dq = dq + dot(doc_turned, dlog_ref[h, :length, part], NN)
            dq_ref[:, r * HD : (r + 1) * HD] = jnp.transpose(dq * SCALE).astype(jnp.bfloat16)

    for_each_length(count_ref[0], keys_ref.shape[0], process)


IN_VMEM = pl.BlockSpec(memory_space=pltpu.VMEM)
IN_SMEM = pl.BlockSpec(memory_space=pltpu.SMEM)
PARAMS = pltpu.CompilerParams(vmem_limit_bytes=16 * 1024 * 1024)


def shape(dims, dtype):
    return jax.ShapeDtypeStruct(dims, dtype)


def cost(queries, pairs, matmuls, extra):
    return pl.CostEstimate(
        flops=2 * HD * pairs * queries * matmuls,
        bytes_accessed=4 * HD * queries + extra,
        transcendentals=pairs * queries,
    )


def leaf_stats(leaf_seg, query, grad_out, leaf_kv):
    rows = query.shape[0]
    heads = leaf_kv.shape[1] // (2 * HD)
    return pl.pallas_call(
        leaf_kernel,
        out_shape=(shape((heads, 3, 8, rows), jnp.float32), shape((rows, rows), jnp.float32)),
        in_specs=[IN_VMEM] * 4,
        out_specs=(IN_VMEM,) * 2,
        compiler_params=PARAMS,
        cost_estimate=cost(rows * heads * GROUPS, rows, 4, 0),
        name="leaf_stats",
    )(leaf_seg, query, grad_out, leaf_kv)


def doc_grads(tok_size, orders, block_parent, leaf_block, query, grad_out, near, far, stats):
    rows = query.shape[0]
    heads = stats.shape[0]
    doc_rows = 2 * near.shape[0]
    return pl.pallas_call(
        functools.partial(doc_kernel, tok_size, orders),
        out_shape=(
            shape(near.shape, jnp.float32),
            shape(far.shape, jnp.bfloat16),
            shape(stats.shape, jnp.float32),
            shape((doc_rows, near.shape[1]), jnp.bfloat16),
            shape((heads, doc_rows, GROUPS * rows), jnp.bfloat16),
            shape((1,), jnp.int32),
        ),
        in_specs=[IN_SMEM] * 2 + [IN_VMEM] * 5,
        out_specs=(IN_VMEM,) * 5 + (IN_SMEM,),
        scratch_shapes=[
            pltpu.SMEM((tok_size,), jnp.int32),
            pltpu.SMEM((tok_size,), jnp.int32),
            pltpu.VMEM((doc_rows, GROUPS * rows), jnp.bfloat16),
            pltpu.VMEM((doc_rows, near.shape[1]), jnp.float32),
        ],
        compiler_params=PARAMS,
        cost_estimate=cost(rows * heads * GROUPS, doc_rows, 4, 0),
        name="doc_grads",
    )(block_parent, leaf_block, query, grad_out, near, far, stats)


def query_grads(first, heads, done, count, query, grad_out, leaf_kv, bias, final, keys, dlog):
    rows = query.shape[0]
    wide = pl.BlockSpec((rows, GROUPS * HD), lambda g: (0, first + g))
    pair = pl.BlockSpec((rows, 2 * HD), lambda g: (0, first + g))
    done = done or []
    return pl.pallas_call(
        functools.partial(query_kernel, first, len(done)),
        out_shape=(shape(query.shape, jnp.bfloat16), shape(leaf_kv.shape, jnp.bfloat16)),
        grid=(heads,),
        in_specs=[IN_SMEM, wide, wide, pair]
        + [IN_VMEM] * 4
        + [pl.BlockSpec(memory_space=pl.ANY)] * len(done),
        out_specs=(wide, pair),
        input_output_aliases={8 + i: i for i in range(len(done))},
        scratch_shapes=[pltpu.VMEM((rows, GROUPS * rows), jnp.bfloat16)] * 2,
        compiler_params=PARAMS,
        cost_estimate=cost(rows * heads * GROUPS, rows, 8, 0),
        name="query_grads",
    )(count, query, grad_out, leaf_kv, bias, final, keys, dlog, *done)


def body(tok_size, head_size, query, leaf_kv, doc_kv, grad_out, block_parent, leaf_block, leaf_seg):
    width = leaf_kv.shape[1]
    orders = hop_orders(tok_size)
    head = lax.axis_index("head")
    swap_head = [(0, 1), (1, 0)]

    def exchange(value, round_index):
        pairs = [(i, i ^ orders[i % 2][round_index]) for i in range(tok_size)]
        return lax.ppermute(value, "tok", pairs)

    def swap_core(value):
        return lax.ppermute(value, "tok", [(i, i ^ 1) for i in range(tok_size)])

    if head_size == 2:
        own = lax.dynamic_slice_in_dim(doc_kv, head * width, width, 1)
        other = lax.dynamic_slice_in_dim(doc_kv, (1 - head) * width, width, 1)
        held = jnp.concatenate([own, lax.ppermute(other, "head", swap_head)], axis=0)
    else:
        held = lax.all_to_all(doc_kv, "head", split_axis=1, concat_axis=0, tiled=True)
    rounds = len(orders[0])
    for r in range(rounds):
        if r < rounds - 1:
            arrived = exchange(held, r)
        else:
            held, own_leaf = lax.optimization_barrier((held, leaf_kv))
            arrived = exchange(held, r)
            stats, bias = leaf_stats(leaf_seg, query, grad_out, own_leaf)
            arrived, stats, bias = lax.optimization_barrier((arrived, stats, bias))
        held = jnp.concatenate([held, arrived], axis=0)
    crossed = swap_core(held)

    total, sent, final, keys, dlog, count = doc_grads(
        tok_size, orders, block_parent, leaf_block, query, grad_out, held, crossed, stats
    )
    total = total + swap_core(sent).astype(jnp.float32)
    heads = final.shape[0]
    calls = min(2, heads)
    done = None
    for step, r in enumerate(reversed(range(rounds))):
        kept = total.shape[0] // 2
        leaving = total[kept:].astype(jnp.bfloat16)
        if step < calls:
            leaving, final = lax.optimization_barrier((leaving, final))
        arrived = exchange(leaving, r)
        if step < calls:
            part = heads // calls
            done = query_grads(
                step * part, part, done, count, query, grad_out, leaf_kv, bias, final, keys, dlog
            )
            arrived, *done = lax.optimization_barrier((arrived, *done))
        total = total[:kept] + arrived.astype(jnp.float32)
    query_grad, leaf_grad = done
    total = total.astype(jnp.bfloat16)
    if head_size == 2:
        kept = total.shape[0] // 2
        mine = total[:kept]
        arrived = lax.ppermute(total[kept:], "head", swap_head)
        doc_grad = jnp.where(
            head == 0,
            jnp.concatenate([mine, arrived], axis=1),
            jnp.concatenate([arrived, mine], axis=1),
        )
    else:
        doc_grad = lax.all_to_all(total, "head", split_axis=0, concat_axis=1, tiled=True)
    return query_grad, leaf_grad, doc_grad


def solution(mesh):
    placed = (
        P("tok", "head"),
        P("tok", "head"),
        P(("tok", "head"), None),
        P("tok", "head"),
        P(),
        P(),
        P("tok", None),
    )
    return jax.shard_map(
        functools.partial(body, mesh.shape["tok"], mesh.shape["head"]),
        mesh=mesh,
        in_specs=placed,
        out_specs=(P("tok", "head"), P("tok", "head"), P(("tok", "head"), None)),
        check_vma=False,
    )
```

```python
import functools

import jax
import jax.numpy as jnp
from jax import lax
from jax.experimental import pallas as pl
from jax.experimental.pallas import tpu as pltpu
from jax.sharding import PartitionSpec as P

QH = 40
KVH = 8
HD = 128
GROUPS = QH // KVH
SCALE = HD ** (-0.5)
LOG2E = 1.4426950408889634
HIDDEN = -1e30
STEPS = 8
NN = (((1,), (0,)), ((), ()))
NT = (((1,), (1,)), ((), ()))
TN = (((0,), (0,)), ((), ()))


def hop_masks(tok_size):
    masks = [1 << b for b in range(tok_size.bit_length() - 1)]
    return masks[:0:-1]


def dot(a, b, dims):
    return lax.dot_general(a, b, dims, preferred_element_type=jnp.float32)


def weights(logit, top):
    return jnp.exp2((logit - top) * (SCALE * LOG2E))


def lanes(h, width, first, size):
    return pl.ds(pl.multiple_of(h * width + first, HD), size)


def prepare_kernel(tok_size, block, parent, leaf_block, seg_ref, bias_ref, place_ref, seen):
    rows = bias_ref.shape[0]
    me = lax.axis_index("tok")

    def clear(i, carry):
        seen[i] = 0
        return carry

    lax.fori_loop(0, tok_size, clear, 0)

    def climb(i, node):
        seen[node] = 1
        return parent[node]

    lax.fori_loop(0, tok_size, climb, leaf_block[me])
    masks = hop_masks(tok_size) + [1]
    total = jnp.int32(0)
    for position in range(tok_size):
        owner = me ^ sum(m for r, m in enumerate(masks) if position >> r & 1)
        visible = seen[owner]
        place_ref[position] = jnp.where(visible == 1, total, -1)
        total = total + visible
    place_ref[tok_size] = total * block

    across = jnp.broadcast_to(seg_ref[...].astype(jnp.float32), (rows, rows))
    down = jnp.transpose(across)
    key = lax.broadcasted_iota(jnp.int32, (rows, rows), 0)
    asker = lax.broadcasted_iota(jnp.int32, (rows, rows), 1)
    bias_ref[...] = jnp.where((across == down) & (key <= asker), 0.0, HIDDEN)


def leaf_kernel(bias_ref, q_ref, go_ref, leaf_ref, stats_ref):
    def one_head(h, carry):
        leaf_keys = leaf_ref[:, lanes(h, 2 * HD, 0, HD)]
        leaf_values = leaf_ref[:, lanes(h, 2 * HD, HD, HD)]
        for r in range(GROUPS):
            cols = lanes(h, GROUPS * HD, r * HD, HD)
            logit = dot(leaf_keys, q_ref[:, cols], NT) + bias_ref[...]
            top = jnp.max(logit, axis=0, keepdims=True)
            weight = weights(logit, top)
            grad_prob = dot(leaf_values, go_ref[:, cols], NT)
            stats_ref[h, 0, r : r + 1, :] = top
            stats_ref[h, 1, r : r + 1, :] = jnp.sum(weight, axis=0, keepdims=True)
            stats_ref[h, 2, r : r + 1, :] = jnp.sum(weight * grad_prob, axis=0, keepdims=True)
        return carry

    lax.fori_loop(0, stats_ref.shape[0], one_head, 0)


def doc_kernel(
    tok_size,
    place,
    q_ref,
    go_ref,
    near_ref,
    far_ref,
    stats_ref,
    dnear_ref,
    dfar_ref,
    final_ref,
    keys_ref,
    dlog_ref,
    prob,
    grads,
):
    rows = q_ref.shape[0]
    heads = stats_ref.shape[0]
    doc_rows = near_ref.shape[0] + far_ref.shape[0]
    half = tok_size // 2
    block = doc_rows // tok_size
    live_rows = place[tok_size]
    keys_ref[...] = jnp.zeros_like(keys_ref)

    for position in range(tok_size):
        source = near_ref if position < half else far_ref
        first = (position % half) * block
        slot = place[position]

        @pl.when(slot >= 0)
        def _(source=source, first=first, slot=slot):
            row = pl.multiple_of(slot * block, block)
            keys_ref[pl.ds(row, block), :] = source[first : first + block, :]

    def process(length):
        body_rows = length - doc_rows // STEPS
        row = body_rows + lax.broadcasted_iota(jnp.int32, (doc_rows // STEPS, 1), 0)
        live = row < live_rows

        def one_head(h, carry):
            doc_keys = keys_ref[:length, lanes(h, 2 * HD, 0, HD)]
            doc_values = keys_ref[:length, lanes(h, 2 * HD, HD, HD)]
            for r in range(GROUPS):
                cols = lanes(h, GROUPS * HD, r * HD, HD)
                logit = dot(doc_keys, q_ref[:, cols], NT)
                tail = jnp.where(live, logit[body_rows:], HIDDEN)
                logit = jnp.concatenate([logit[:body_rows], tail], axis=0) if body_rows else tail
                leaf_top = stats_ref[h, 0, r : r + 1, :]
                top = jnp.maximum(leaf_top, jnp.max(logit, axis=0, keepdims=True))
                shrink = weights(leaf_top, top)
                weight = weights(logit, top)
                leaf_sum = stats_ref[h, 1, r : r + 1, :] * shrink
                leaf_dot = stats_ref[h, 2, r : r + 1, :] * shrink
                inverse = 1.0 / (leaf_sum + jnp.sum(weight, axis=0, keepdims=True))
                grad_prob = dot(doc_values, go_ref[:, cols], NT)
                grad_dot = leaf_dot + jnp.sum(weight * grad_prob, axis=0, keepdims=True)
                grad_dot = grad_dot * inverse
                probability = weight * inverse
                prob[:length, r * rows : (r + 1) * rows] = probability.astype(jnp.bfloat16)
                grad_logit = (probability * (grad_prob - grad_dot)).astype(jnp.bfloat16)
                dlog_ref[h, :length, r * rows : (r + 1) * rows] = grad_logit
                final_ref[h, 0, r : r + 1, :] = top
                final_ref[h, 1, r : r + 1, :] = inverse
                final_ref[h, 2, r : r + 1, :] = grad_dot
            q_all = stacked(q_ref, h)
            go_all = stacked(go_ref, h)
            grad_key = dot(dlog_ref[h, :length, :], q_all, NN) * SCALE
            grads[:length, lanes(h, 2 * HD, 0, HD)] = grad_key
            grads[:length, lanes(h, 2 * HD, HD, HD)] = dot(prob[:length, :], go_all, NN)
            return carry

        lax.fori_loop(0, heads, one_head, 0)

    for_each_length(live_rows, doc_rows, process)

    for position in range(tok_size):
        target = dnear_ref if position < half else dfar_ref
        first = (position % half) * block
        slot = place[position]

        @pl.when(slot >= 0)
        def _(target=target, first=first, slot=slot):
            row = pl.multiple_of(slot * block, block)
            target[first : first + block, :] = grads[pl.ds(row, block), :].astype(target.dtype)

        @pl.when(slot < 0)
        def _(target=target, first=first):
            target[first : first + block, :] = jnp.zeros((block, target.shape[1]), target.dtype)


def stacked(ref, h):
    return jnp.concatenate([ref[:, lanes(h, GROUPS * HD, r * HD, HD)] for r in range(GROUPS)], axis=0)


def for_each_length(live_rows, doc_rows, process):
    lengths = [doc_rows // STEPS * (k + 1) for k in range(STEPS)]
    for low, length in zip([0] + lengths, lengths):

        @pl.when((live_rows > low) & (live_rows <= length))
        def _(length=length):
            process(length)


def query_kernel(
    first_head,
    n_done,
    place,
    q_ref,
    go_ref,
    leaf_ref,
    bias_ref,
    final_ref,
    keys_ref,
    dlog_ref,
    *rest,
):
    dq_ref, dleaf_ref, prob, dlog = rest[n_done:]
    h = first_head + pl.program_id(0)
    rows = q_ref.shape[0]
    leaf_keys = leaf_ref[:, lanes(h, 2 * HD, 0, HD)]
    leaf_values = leaf_ref[:, lanes(h, 2 * HD, HD, HD)]
    leaf_turned = jnp.transpose(leaf_keys)
    for r in range(GROUPS):
        cols = lanes(h, GROUPS * HD, r * HD, HD)
        logit = dot(leaf_keys, q_ref[:, cols], NT) + bias_ref[...]
        probability = weights(logit, final_ref[h, 0, r : r + 1, :]) * final_ref[h, 1, r : r + 1, :]
        grad_prob = dot(leaf_values, go_ref[:, cols], NT)
        grad_logit = probability * (grad_prob - final_ref[h, 2, r : r + 1, :])
        prob[:, r * rows : (r + 1) * rows] = probability.astype(jnp.bfloat16)
        dlog[:, r * rows : (r + 1) * rows] = grad_logit.astype(jnp.bfloat16)
    grad_key = dot(dlog[...], stacked(q_ref, h), NN) * SCALE
    dleaf_ref[:, :HD] = grad_key.astype(jnp.bfloat16)
    dleaf_ref[:, HD:] = dot(prob[...], stacked(go_ref, h), NN).astype(jnp.bfloat16)

    def process(length):
        doc_turned = jnp.transpose(keys_ref[:length, lanes(h, 2 * HD, 0, HD)])
        for r in range(GROUPS):
            part = slice(r * rows, (r + 1) * rows)
            dq = dot(leaf_turned, dlog[:, part], NN)
            dq = dq + dot(doc_turned, dlog_ref[h, :length, part], NN)
            dq_ref[:, r * HD : (r + 1) * HD] = jnp.transpose(dq * SCALE).astype(jnp.bfloat16)

    for_each_length(place[place.shape[0] - 1], keys_ref.shape[0], process)


IN_VMEM = pl.BlockSpec(memory_space=pltpu.VMEM)
IN_SMEM = pl.BlockSpec(memory_space=pltpu.SMEM)
PARAMS = pltpu.CompilerParams(vmem_limit_bytes=16 * 1024 * 1024)


def shape(dims, dtype):
    return jax.ShapeDtypeStruct(dims, dtype)


def cost(queries, pairs, matmuls, extra):
    return pl.CostEstimate(
        flops=2 * HD * pairs * queries * matmuls,
        bytes_accessed=4 * HD * queries + extra,
        transcendentals=pairs * queries,
    )


def prepare(tok_size, block, block_parent, leaf_block, leaf_seg):
    rows = leaf_seg.shape[1]
    return pl.pallas_call(
        functools.partial(prepare_kernel, tok_size, block),
        out_shape=(shape((rows, rows), jnp.float32), shape((tok_size + 1,), jnp.int32)),
        in_specs=[IN_SMEM, IN_SMEM, IN_VMEM],
        out_specs=(IN_VMEM, IN_SMEM),
        scratch_shapes=[pltpu.SMEM((tok_size,), jnp.int32)],
        compiler_params=PARAMS,
        cost_estimate=cost(rows, rows, 1, 0),
        name="prepare",
    )(block_parent, leaf_block, leaf_seg)


def leaf_stats(bias, query, grad_out, leaf_kv):
    rows = query.shape[0]
    heads = leaf_kv.shape[1] // (2 * HD)
    return pl.pallas_call(
        leaf_kernel,
        out_shape=shape((heads, 3, 8, rows), jnp.float32),
        in_specs=[IN_VMEM] * 4,
        out_specs=IN_VMEM,
        compiler_params=PARAMS,
        cost_estimate=cost(rows * heads * GROUPS, rows, 4, 0),
        name="leaf_stats",
    )(bias, query, grad_out, leaf_kv)


def doc_grads(tok_size, place, query, grad_out, near, far, stats):
    rows = query.shape[0]
    heads = stats.shape[0]
    doc_rows = 2 * near.shape[0]
    return pl.pallas_call(
        functools.partial(doc_kernel, tok_size),
        out_shape=(
            shape(near.shape, jnp.float32),
            shape(far.shape, jnp.bfloat16),
            shape(stats.shape, jnp.float32),
            shape((doc_rows, near.shape[1]), jnp.bfloat16),
            shape((heads, doc_rows, GROUPS * rows), jnp.bfloat16),
        ),
        in_specs=[IN_SMEM] + [IN_VMEM] * 5,
        out_specs=(IN_VMEM,) * 5,
        scratch_shapes=[
            pltpu.VMEM((doc_rows, GROUPS * rows), jnp.bfloat16),
            pltpu.VMEM((doc_rows, near.shape[1]), jnp.float32),
        ],
        compiler_params=PARAMS,
        cost_estimate=cost(rows * heads * GROUPS, doc_rows, 4, 0),
        name="doc_grads",
    )(place, query, grad_out, near, far, stats)


def query_grads(first, heads, done, place, query, grad_out, leaf_kv, bias, final, keys, dlog):
    rows = query.shape[0]
    wide = pl.BlockSpec((rows, GROUPS * HD), lambda g: (0, first + g))
    pair = pl.BlockSpec((rows, 2 * HD), lambda g: (0, first + g))
    return pl.pallas_call(
        functools.partial(query_kernel, first, len(done)),
        out_shape=(shape(query.shape, jnp.bfloat16), shape(leaf_kv.shape, jnp.bfloat16)),
        grid=(heads,),
        in_specs=[IN_SMEM] + [IN_VMEM] * 7 + [pl.BlockSpec(memory_space=pl.ANY)] * len(done),
        out_specs=(wide, pair),
        input_output_aliases={8 + i: i for i in range(len(done))},
        scratch_shapes=[pltpu.VMEM((rows, GROUPS * rows), jnp.bfloat16)] * 2,
        compiler_params=PARAMS,
        cost_estimate=cost(rows * heads * GROUPS, rows, 8, 0),
        name="query_grads",
    )(place, query, grad_out, leaf_kv, bias, final, keys, dlog, *done)


def body(tok_size, head_size, query, leaf_kv, doc_kv, grad_out, block_parent, leaf_block, leaf_seg):
    width = leaf_kv.shape[1]
    block = doc_kv.shape[0] * head_size
    masks = hop_masks(tok_size)
    rounds = len(masks)
    head = lax.axis_index("head")
    swap_head = [(0, 1), (1, 0)]

    def exchange(value, mask):
        return lax.ppermute(value, "tok", [(i, i ^ mask) for i in range(tok_size)])

    if head_size == 2:
        both = jnp.concatenate([doc_kv, lax.ppermute(doc_kv, "head", swap_head)], axis=0)
        held = lax.dynamic_slice_in_dim(both, head * width, width, 1)
    else:
        held = lax.all_to_all(doc_kv, "head", split_axis=1, concat_axis=0, tiled=True)
    resident = (query, grad_out, leaf_kv)
    for r, mask in enumerate(masks):
        if r == 0:
            held, leaf_seg = lax.optimization_barrier((held, leaf_seg))
        if r == rounds - 1:
            held, bias = lax.optimization_barrier((held, bias))
        arrived = exchange(held, mask)
        if r == 0:
            early = prepare(tok_size, block, block_parent, leaf_block, leaf_seg)
            arrived, (bias, place) = lax.optimization_barrier((arrived, early))
        if r == rounds - 1:
            arrived, stats = lax.optimization_barrier((arrived, leaf_stats(bias, *resident)))
        held = jnp.concatenate([held, arrived], axis=0)
    crossed = exchange(held, 1)

    total, sent, final, keys, dlog = doc_grads(tok_size, place, *resident[:2], held, crossed, stats)
    total = total + exchange(sent, 1).astype(jnp.float32)
    heads = final.shape[0]
    parts = [2, 1, 1] if heads == 4 else [heads]
    done = []
    for step in range(rounds):
        kept = total.shape[0] // 2
        leaving = total[kept:].astype(jnp.bfloat16)
        if step < len(parts):
            leaving, final = lax.optimization_barrier((leaving, final))
        arrived = exchange(leaving, masks[rounds - 1 - step])
        if step < len(parts):
            first = sum(parts[:step])
            done = query_grads(
                first, parts[step], done, place, *resident, bias, final, keys, dlog
            )
            arrived, done = lax.optimization_barrier((arrived, done))
        total = total[:kept] + arrived.astype(jnp.float32)
    query_grad, leaf_grad = done
    total = total.astype(jnp.bfloat16)
    if head_size == 2:
        kept = total.shape[0] // 2
        mine = total[:kept]
        arrived = lax.ppermute(total[kept:], "head", swap_head)
        doc_grad = jnp.where(
            head == 0,
            jnp.concatenate([mine, arrived], axis=1),
            jnp.concatenate([arrived, mine], axis=1),
        )
    else:
        doc_grad = lax.all_to_all(total, "head", split_axis=0, concat_axis=1, tiled=True)
    return query_grad, leaf_grad, doc_grad


def solution(mesh):
    placed = (
        P("tok", "head"),
        P("tok", "head"),
        P(("tok", "head"), None),
        P("tok", "head"),
        P(),
        P(),
        P("tok", None),
    )
    return jax.shard_map(
        functools.partial(body, mesh.shape["tok"], mesh.shape["head"]),
        mesh=mesh,
        in_specs=placed,
        out_specs=(P("tok", "head"), P("tok", "head"), P(("tok", "head"), None)),
        check_vma=False,
    )
```

```python
import functools

import jax
import jax.numpy as jnp
from jax import lax
from jax.experimental import pallas as pl
from jax.experimental.pallas import tpu as pltpu
from jax.sharding import PartitionSpec as P

QH = 40
KVH = 8
HD = 128
GROUPS = QH // KVH
SCALE = HD ** (-0.5)
LOG2E = 1.4426950408889634
HIDDEN = -1e30
STEPS = 8
NN = (((1,), (0,)), ((), ()))
NT = (((1,), (1,)), ((), ()))
TN = (((0,), (0,)), ((), ()))


def hop_orders(tok_size):
    masks = [1 << b for b in range(tok_size.bit_length() - 1)]
    far = masks[:0:-1]
    other = far if len(far) < 3 else far[:-2] + [far[-1], far[-2]]
    return far, other


def dot(a, b, dims):
    return lax.dot_general(a, b, dims, preferred_element_type=jnp.float32)


def weights(logit, top):
    return jnp.exp2((logit - top) * (SCALE * LOG2E))


def lanes(h, width, first, size):
    return pl.ds(pl.multiple_of(h * width + first, HD), size)


def prepare_kernel(tok_size, block, parent, leaf_block, seg_ref, bias_ref, place_ref, seen):
    rows = bias_ref.shape[0]
    me = lax.axis_index("tok")

    def clear(i, carry):
        seen[i] = 0
        return carry

    lax.fori_loop(0, tok_size, clear, 0)

    def climb(i, node):
        seen[node] = 1
        return parent[node]

    lax.fori_loop(0, tok_size, climb, leaf_block[me])
    orders = hop_orders(tok_size)
    core = lax.rem(me, 2)
    half = tok_size // 2
    total = jnp.int32(0)
    for position in range(tok_size):
        local = position % half
        same = sum(m for r, m in enumerate(orders[0]) if local >> r & 1)
        cross = sum(m for r, m in enumerate(orders[1]) if local >> r & 1)
        if position < half:
            owner = me ^ jnp.where(core == 0, same, cross)
        else:
            owner = me ^ 1 ^ jnp.where(core == 0, cross, same)
        visible = seen[owner]
        place_ref[position] = jnp.where(visible == 1, total, -1)
        total = total + visible
    place_ref[tok_size] = total * block

    across = jnp.broadcast_to(seg_ref[...].astype(jnp.float32), (rows, rows))
    down = jnp.transpose(across)
    key = lax.broadcasted_iota(jnp.int32, (rows, rows), 0)
    asker = lax.broadcasted_iota(jnp.int32, (rows, rows), 1)
    bias_ref[...] = jnp.where((across == down) & (key <= asker), 0.0, HIDDEN)


def leaf_kernel(bias_ref, q_ref, go_ref, leaf_ref, stats_ref):
    def one_head(h, carry):
        leaf_keys = leaf_ref[:, lanes(h, 2 * HD, 0, HD)]
        leaf_values = leaf_ref[:, lanes(h, 2 * HD, HD, HD)]
        for r in range(GROUPS):
            cols = lanes(h, GROUPS * HD, r * HD, HD)
            logit = dot(leaf_keys, q_ref[:, cols], NT) + bias_ref[...]
            top = jnp.max(logit, axis=0, keepdims=True)
            weight = weights(logit, top)
            grad_prob = dot(leaf_values, go_ref[:, cols], NT)
            stats_ref[h, 0, r : r + 1, :] = top
            stats_ref[h, 1, r : r + 1, :] = jnp.sum(weight, axis=0, keepdims=True)
            stats_ref[h, 2, r : r + 1, :] = jnp.sum(weight * grad_prob, axis=0, keepdims=True)
        return carry

    lax.fori_loop(0, stats_ref.shape[0], one_head, 0)


def doc_kernel(
    tok_size,
    place,
    q_ref,
    go_ref,
    near_ref,
    far_ref,
    stats_ref,
    dnear_ref,
    dfar_ref,
    final_ref,
    keys_ref,
    dlog_ref,
    prob,
    grads,
):
    rows = q_ref.shape[0]
    heads = stats_ref.shape[0]
    doc_rows = near_ref.shape[0] + far_ref.shape[0]
    half = tok_size // 2
    block = doc_rows // tok_size
    live_rows = place[tok_size]
    keys_ref[...] = jnp.zeros_like(keys_ref)

    for position in range(tok_size):
        source = near_ref if position < half else far_ref
        first = (position % half) * block
        slot = place[position]

        @pl.when(slot >= 0)
        def _(source=source, first=first, slot=slot):
            row = pl.multiple_of(slot * block, block)
            keys_ref[pl.ds(row, block), :] = source[first : first + block, :]

    def process(length):
        body_rows = length - doc_rows // STEPS
        row = body_rows + lax.broadcasted_iota(jnp.int32, (doc_rows // STEPS, 1), 0)
        live = row < live_rows

        def one_head(h, carry):
            doc_keys = keys_ref[:length, lanes(h, 2 * HD, 0, HD)]
            doc_values = keys_ref[:length, lanes(h, 2 * HD, HD, HD)]
            for r in range(GROUPS):
                cols = lanes(h, GROUPS * HD, r * HD, HD)
                logit = dot(doc_keys, q_ref[:, cols], NT)
                tail = jnp.where(live, logit[body_rows:], HIDDEN)
                logit = jnp.concatenate([logit[:body_rows], tail], axis=0) if body_rows else tail
                leaf_top = stats_ref[h, 0, r : r + 1, :]
                top = jnp.maximum(leaf_top, jnp.max(logit, axis=0, keepdims=True))
                shrink = weights(leaf_top, top)
                weight = weights(logit, top)
                leaf_sum = stats_ref[h, 1, r : r + 1, :] * shrink
                leaf_dot = stats_ref[h, 2, r : r + 1, :] * shrink
                inverse = 1.0 / (leaf_sum + jnp.sum(weight, axis=0, keepdims=True))
                grad_prob = dot(doc_values, go_ref[:, cols], NT)
                grad_dot = leaf_dot + jnp.sum(weight * grad_prob, axis=0, keepdims=True)
                grad_dot = grad_dot * inverse
                probability = weight * inverse
                prob[:length, r * rows : (r + 1) * rows] = probability.astype(jnp.bfloat16)
                grad_logit = (probability * (grad_prob - grad_dot)).astype(jnp.bfloat16)
                dlog_ref[h, :length, r * rows : (r + 1) * rows] = grad_logit
                final_ref[h, 0, r : r + 1, :] = top
                final_ref[h, 1, r : r + 1, :] = inverse
                final_ref[h, 2, r : r + 1, :] = grad_dot
            q_all = stacked(q_ref, h)
            go_all = stacked(go_ref, h)
            grad_key = dot(dlog_ref[h, :length, :], q_all, NN) * SCALE
            grads[:length, lanes(h, 2 * HD, 0, HD)] = grad_key
            grads[:length, lanes(h, 2 * HD, HD, HD)] = dot(prob[:length, :], go_all, NN)
            return carry

        lax.fori_loop(0, heads, one_head, 0)

    for_each_length(live_rows, doc_rows, process)

    for position in range(tok_size):
        target = dnear_ref if position < half else dfar_ref
        first = (position % half) * block
        slot = place[position]

        @pl.when(slot >= 0)
        def _(target=target, first=first, slot=slot):
            row = pl.multiple_of(slot * block, block)
            target[first : first + block, :] = grads[pl.ds(row, block), :].astype(target.dtype)

        @pl.when(slot < 0)
        def _(target=target, first=first):
            target[first : first + block, :] = jnp.zeros((block, target.shape[1]), target.dtype)


def stacked(ref, h):
    return jnp.concatenate([ref[:, lanes(h, GROUPS * HD, r * HD, HD)] for r in range(GROUPS)], axis=0)


def for_each_length(live_rows, doc_rows, process):
    lengths = [doc_rows // STEPS * (k + 1) for k in range(STEPS)]
    for low, length in zip([0] + lengths, lengths):

        @pl.when((live_rows > low) & (live_rows <= length))
        def _(length=length):
            process(length)


def query_kernel(
    first_head,
    n_done,
    place,
    q_ref,
    go_ref,
    leaf_ref,
    bias_ref,
    final_ref,
    keys_ref,
    dlog_ref,
    *rest,
):
    dq_ref, dleaf_ref, prob, dlog = rest[n_done:]
    h = first_head + pl.program_id(0)
    rows = q_ref.shape[0]
    leaf_keys = leaf_ref[:, lanes(h, 2 * HD, 0, HD)]
    leaf_values = leaf_ref[:, lanes(h, 2 * HD, HD, HD)]
    leaf_turned = jnp.transpose(leaf_keys)
    for r in range(GROUPS):
        cols = lanes(h, GROUPS * HD, r * HD, HD)
        logit = dot(leaf_keys, q_ref[:, cols], NT) + bias_ref[...]
        probability = weights(logit, final_ref[h, 0, r : r + 1, :]) * final_ref[h, 1, r : r + 1, :]
        grad_prob = dot(leaf_values, go_ref[:, cols], NT)
        grad_logit = probability * (grad_prob - final_ref[h, 2, r : r + 1, :])
        prob[:, r * rows : (r + 1) * rows] = probability.astype(jnp.bfloat16)
        dlog[:, r * rows : (r + 1) * rows] = grad_logit.astype(jnp.bfloat16)
    grad_key = dot(dlog[...], stacked(q_ref, h), NN) * SCALE
    dleaf_ref[:, :HD] = grad_key.astype(jnp.bfloat16)
    dleaf_ref[:, HD:] = dot(prob[...], stacked(go_ref, h), NN).astype(jnp.bfloat16)

    def process(length):
        doc_turned = jnp.transpose(keys_ref[:length, lanes(h, 2 * HD, 0, HD)])
        for r in range(GROUPS):
            part = slice(r * rows, (r + 1) * rows)
            dq = dot(leaf_turned, dlog[:, part], NN)
            dq = dq + dot(doc_turned, dlog_ref[h, :length, part], NN)
            dq_ref[:, r * HD : (r + 1) * HD] = jnp.transpose(dq * SCALE).astype(jnp.bfloat16)

    for_each_length(place[place.shape[0] - 1], keys_ref.shape[0], process)


IN_VMEM = pl.BlockSpec(memory_space=pltpu.VMEM)
IN_SMEM = pl.BlockSpec(memory_space=pltpu.SMEM)
PARAMS = pltpu.CompilerParams(vmem_limit_bytes=16 * 1024 * 1024)


def shape(dims, dtype):
    return jax.ShapeDtypeStruct(dims, dtype)


def cost(queries, pairs, matmuls, extra):
    return pl.CostEstimate(
        flops=2 * HD * pairs * queries * matmuls,
        bytes_accessed=4 * HD * queries + extra,
        transcendentals=pairs * queries,
    )


def prepare(tok_size, block, block_parent, leaf_block, leaf_seg):
    rows = leaf_seg.shape[1]
    return pl.pallas_call(
        functools.partial(prepare_kernel, tok_size, block),
        out_shape=(shape((rows, rows), jnp.float32), shape((tok_size + 1,), jnp.int32)),
        in_specs=[IN_SMEM, IN_SMEM, IN_VMEM],
        out_specs=(IN_VMEM, IN_SMEM),
        scratch_shapes=[pltpu.SMEM((tok_size,), jnp.int32)],
        compiler_params=PARAMS,
        cost_estimate=cost(rows, rows, 1, 0),
        name="prepare",
    )(block_parent, leaf_block, leaf_seg)


def leaf_stats(bias, query, grad_out, leaf_kv):
    rows = query.shape[0]
    heads = leaf_kv.shape[1] // (2 * HD)
    return pl.pallas_call(
        leaf_kernel,
        out_shape=shape((heads, 3, 8, rows), jnp.float32),
        in_specs=[IN_VMEM] * 4,
        out_specs=IN_VMEM,
        compiler_params=PARAMS,
        cost_estimate=cost(rows * heads * GROUPS, rows, 4, 0),
        name="leaf_stats",
    )(bias, query, grad_out, leaf_kv)


def doc_grads(tok_size, place, query, grad_out, near, far, stats):
    rows = query.shape[0]
    heads = stats.shape[0]
    doc_rows = 2 * near.shape[0]
    return pl.pallas_call(
        functools.partial(doc_kernel, tok_size),
        out_shape=(
            shape(near.shape, jnp.float32),
            shape(far.shape, jnp.bfloat16),
            shape(stats.shape, jnp.float32),
            shape((doc_rows, near.shape[1]), jnp.bfloat16),
            shape((heads, doc_rows, GROUPS * rows), jnp.bfloat16),
        ),
        in_specs=[IN_SMEM] + [IN_VMEM] * 5,
        out_specs=(IN_VMEM,) * 5,
        scratch_shapes=[
            pltpu.VMEM((doc_rows, GROUPS * rows), jnp.bfloat16),
            pltpu.VMEM((doc_rows, near.shape[1]), jnp.float32),
        ],
        compiler_params=PARAMS,
        cost_estimate=cost(rows * heads * GROUPS, doc_rows, 4, 0),
        name="doc_grads",
    )(place, query, grad_out, near, far, stats)


def query_grads(first, heads, done, place, query, grad_out, leaf_kv, bias, final, keys, dlog):
    rows = query.shape[0]
    wide = pl.BlockSpec((rows, GROUPS * HD), lambda g: (0, first + g))
    pair = pl.BlockSpec((rows, 2 * HD), lambda g: (0, first + g))
    return pl.pallas_call(
        functools.partial(query_kernel, first, len(done)),
        out_shape=(shape(query.shape, jnp.bfloat16), shape(leaf_kv.shape, jnp.bfloat16)),
        grid=(heads,),
        in_specs=[IN_SMEM] + [IN_VMEM] * 7 + [pl.BlockSpec(memory_space=pl.ANY)] * len(done),
        out_specs=(wide, pair),
        input_output_aliases={8 + i: i for i in range(len(done))},
        scratch_shapes=[pltpu.VMEM((rows, GROUPS * rows), jnp.bfloat16)] * 2,
        compiler_params=PARAMS,
        cost_estimate=cost(rows * heads * GROUPS, rows, 8, 0),
        name="query_grads",
    )(place, query, grad_out, leaf_kv, bias, final, keys, dlog, *done)


def body(tok_size, head_size, query, leaf_kv, doc_kv, grad_out, block_parent, leaf_block, leaf_seg):
    width = leaf_kv.shape[1]
    block = doc_kv.shape[0] * head_size
    orders = hop_orders(tok_size)
    rounds = len(orders[0])
    head = lax.axis_index("head")
    swap_head = [(0, 1), (1, 0)]

    def exchange(value, r):
        return lax.ppermute(value, "tok", [(i, i ^ orders[i % 2][r]) for i in range(tok_size)])

    def swap_core(value):
        return lax.ppermute(value, "tok", [(i, i ^ 1) for i in range(tok_size)])

    if head_size == 2:
        arrived = lax.ppermute(doc_kv, "head", swap_head)
        own = lax.dynamic_slice_in_dim(doc_kv, head * width, width, 1)
        arrived, own = lax.optimization_barrier((arrived, own))
        arrived = lax.dynamic_slice_in_dim(arrived, head * width, width, 1)
        held = jnp.concatenate([own, arrived], axis=0)
    else:
        held = lax.all_to_all(doc_kv, "head", split_axis=1, concat_axis=0, tiled=True)
    resident = (query, grad_out, leaf_kv)
    early_round = max(0, rounds - 2)
    for r in range(rounds):
        if r == early_round:
            held, leaf_seg = lax.optimization_barrier((held, leaf_seg))
        if r == rounds - 1:
            held, bias = lax.optimization_barrier((held, bias))
        arrived = exchange(held, r)
        if r == early_round:
            early = prepare(tok_size, block, block_parent, leaf_block, leaf_seg)
            arrived, (bias, place) = lax.optimization_barrier((arrived, early))
        if r == rounds - 1:
            arrived, stats = lax.optimization_barrier((arrived, leaf_stats(bias, *resident)))
        held = jnp.concatenate([held, arrived], axis=0)
    crossed = swap_core(held)

    total, sent, final, keys, dlog = doc_grads(tok_size, place, *resident[:2], held, crossed, stats)
    total = total + swap_core(sent).astype(jnp.float32)
    heads = final.shape[0]
    parts = [2, 1, 1] if heads == 4 else [heads]
    done = []
    for step in range(rounds):
        kept = total.shape[0] // 2
        leaving = total[kept:].astype(jnp.bfloat16)
        if step < len(parts):
            leaving, final = lax.optimization_barrier((leaving, final))
        arrived = exchange(leaving, rounds - 1 - step)
        if step < len(parts):
            first = sum(parts[:step])
            done = query_grads(
                first, parts[step], done, place, *resident, bias, final, keys, dlog
            )
            arrived, done = lax.optimization_barrier((arrived, done))
        total = total[:kept] + arrived.astype(jnp.float32)
    query_grad, leaf_grad = done
    total = total.astype(jnp.bfloat16)
    if head_size == 2:
        kept = total.shape[0] // 2
        mine = total[:kept]
        arrived = lax.ppermute(total[kept:], "head", swap_head)
        doc_grad = jnp.where(
            head == 0,
            jnp.concatenate([mine, arrived], axis=1),
            jnp.concatenate([arrived, mine], axis=1),
        )
    else:
        doc_grad = lax.all_to_all(total, "head", split_axis=0, concat_axis=1, tiled=True)
    return query_grad, leaf_grad, doc_grad


def solution(mesh):
    placed = (
        P("tok", "head"),
        P("tok", "head"),
        P(("tok", "head"), None),
        P("tok", "head"),
        P(),
        P(),
        P("tok", None),
    )
    return jax.shard_map(
        functools.partial(body, mesh.shape["tok"], mesh.shape["head"]),
        mesh=mesh,
        in_specs=placed,
        out_specs=(P("tok", "head"), P("tok", "head"), P(("tok", "head"), None)),
        check_vma=False,
    )
```

```python
import functools

import jax
import jax.numpy as jnp
from jax import lax
from jax.experimental import pallas as pl
from jax.experimental.pallas import tpu as pltpu
from jax.sharding import PartitionSpec as P

QH = 40
KVH = 8
HD = 128
GROUPS = QH // KVH
SCALE = HD ** (-0.5)
LOG2E = 1.4426950408889634
HIDDEN = -1e30
STEPS = 8
NN = (((1,), (0,)), ((), ()))
NT = (((1,), (1,)), ((), ()))
TN = (((0,), (0,)), ((), ()))


def hop_orders(tok_size):
    masks = [1 << b for b in range(tok_size.bit_length() - 1)]
    far = masks[:0:-1]
    other = far if len(far) < 3 else far[:-2] + [far[-1], far[-2]]
    return far, other


def dot(a, b, dims):
    return lax.dot_general(a, b, dims, preferred_element_type=jnp.float32)


def weights(logit, top):
    return jnp.exp2((logit - top) * (SCALE * LOG2E))


def lanes(h, width, first, size):
    return pl.ds(pl.multiple_of(h * width + first, HD), size)


def prepare_kernel(tok_size, block, parent, leaf_block, seg_ref, bias_ref, place_ref, seen):
    rows = bias_ref.shape[0]
    me = lax.axis_index("tok")

    def clear(i, carry):
        seen[i] = 0
        return carry

    lax.fori_loop(0, tok_size, clear, 0)

    def climb(i, node):
        seen[node] = 1
        return parent[node]

    lax.fori_loop(0, tok_size, climb, leaf_block[me])
    orders = hop_orders(tok_size)
    core = lax.rem(me, 2)
    half = tok_size // 2
    total = jnp.int32(0)
    for position in range(tok_size):
        local = position % half
        same = sum(m for r, m in enumerate(orders[0]) if local >> r & 1)
        cross = sum(m for r, m in enumerate(orders[1]) if local >> r & 1)
        if position < half:
            owner = me ^ jnp.where(core == 0, same, cross)
        else:
            owner = me ^ 1 ^ jnp.where(core == 0, cross, same)
        visible = seen[owner]
        place_ref[position] = jnp.where(visible == 1, total, -1)
        total = total + visible
    place_ref[tok_size] = total * block

    across = jnp.broadcast_to(seg_ref[...].astype(jnp.float32), (rows, rows))
    down = jnp.transpose(across)
    key = lax.broadcasted_iota(jnp.int32, (rows, rows), 0)
    asker = lax.broadcasted_iota(jnp.int32, (rows, rows), 1)
    bias_ref[...] = jnp.where((across == down) & (key <= asker), 0.0, HIDDEN)


def leaf_kernel(bias_ref, q_ref, go_ref, leaf_ref, stats_ref):
    def one_head(h, carry):
        leaf_keys = leaf_ref[:, lanes(h, 2 * HD, 0, HD)]
        leaf_values = leaf_ref[:, lanes(h, 2 * HD, HD, HD)]
        for r in range(GROUPS):
            cols = lanes(h, GROUPS * HD, r * HD, HD)
            logit = dot(leaf_keys, q_ref[:, cols], NT) + bias_ref[...]
            top = jnp.max(logit, axis=0, keepdims=True)
            weight = weights(logit, top)
            grad_prob = dot(leaf_values, go_ref[:, cols], NT)
            stats_ref[h, 0, r : r + 1, :] = top
            stats_ref[h, 1, r : r + 1, :] = jnp.sum(weight, axis=0, keepdims=True)
            stats_ref[h, 2, r : r + 1, :] = jnp.sum(weight * grad_prob, axis=0, keepdims=True)
        return carry

    lax.fori_loop(0, stats_ref.shape[0], one_head, 0)


def doc_kernel(
    tok_size,
    place,
    q_ref,
    go_ref,
    near_ref,
    far_ref,
    stats_ref,
    dnear_ref,
    dfar_ref,
    final_ref,
    keys_ref,
    dlog_ref,
    prob,
    grads,
):
    rows = q_ref.shape[0]
    heads = stats_ref.shape[0]
    doc_rows = near_ref.shape[0] + far_ref.shape[0]
    half = tok_size // 2
    block = doc_rows // tok_size
    live_rows = place[tok_size]
    for spare in range(doc_rows // STEPS // block - 1):

        @pl.when(live_rows + spare * block < doc_rows)
        def _(spare=spare):
            row = pl.multiple_of(live_rows + spare * block, block)
            keys_ref[pl.ds(row, block), :] = jnp.zeros((block, keys_ref.shape[1]), keys_ref.dtype)

    for position in range(tok_size):
        source = near_ref if position < half else far_ref
        first = (position % half) * block
        slot = place[position]

        @pl.when(slot >= 0)
        def _(source=source, first=first, slot=slot):
            row = pl.multiple_of(slot * block, block)
            keys_ref[pl.ds(row, block), :] = source[first : first + block, :]

    def process(length):
        body_rows = length - doc_rows // STEPS
        row = body_rows + lax.broadcasted_iota(jnp.int32, (doc_rows // STEPS, 1), 0)
        live = row < live_rows

        def one_head(h, carry):
            doc_keys = keys_ref[:length, lanes(h, 2 * HD, 0, HD)]
            doc_values = keys_ref[:length, lanes(h, 2 * HD, HD, HD)]
            for r in range(GROUPS):
                cols = lanes(h, GROUPS * HD, r * HD, HD)
                logit = dot(doc_keys, q_ref[:, cols], NT)
                tail = jnp.where(live, logit[body_rows:], HIDDEN)
                logit = jnp.concatenate([logit[:body_rows], tail], axis=0) if body_rows else tail
                leaf_top = stats_ref[h, 0, r : r + 1, :]
                top = jnp.maximum(leaf_top, jnp.max(logit, axis=0, keepdims=True))
                shrink = weights(leaf_top, top)
                weight = weights(logit, top)
                leaf_sum = stats_ref[h, 1, r : r + 1, :] * shrink
                leaf_dot = stats_ref[h, 2, r : r + 1, :] * shrink
                inverse = 1.0 / (leaf_sum + jnp.sum(weight, axis=0, keepdims=True))
                grad_prob = dot(doc_values, go_ref[:, cols], NT)
                grad_dot = leaf_dot + jnp.sum(weight * grad_prob, axis=0, keepdims=True)
                grad_dot = grad_dot * inverse
                probability = weight * inverse
                prob[:length, r * rows : (r + 1) * rows] = probability.astype(jnp.bfloat16)
                grad_logit = (probability * (grad_prob - grad_dot)).astype(jnp.bfloat16)
                dlog_ref[h, :length, r * rows : (r + 1) * rows] = grad_logit
                final_ref[h, 0, r : r + 1, :] = top
                final_ref[h, 1, r : r + 1, :] = inverse
                final_ref[h, 2, r : r + 1, :] = grad_dot
            q_all = stacked(q_ref, h)
            go_all = stacked(go_ref, h)
            grad_key = dot(dlog_ref[h, :length, :], q_all, NN) * SCALE
            grads[:length, lanes(h, 2 * HD, 0, HD)] = grad_key
            grads[:length, lanes(h, 2 * HD, HD, HD)] = dot(prob[:length, :], go_all, NN)
            return carry

        lax.fori_loop(0, heads, one_head, 0)

    for_each_length(live_rows, doc_rows, process)

    for position in range(tok_size):
        target = dnear_ref if position < half else dfar_ref
        first = (position % half) * block
        slot = place[position]

        @pl.when(slot >= 0)
        def _(target=target, first=first, slot=slot):
            row = pl.multiple_of(slot * block, block)
            target[first : first + block, :] = grads[pl.ds(row, block), :].astype(target.dtype)

        @pl.when(slot < 0)
        def _(target=target, first=first):
            target[first : first + block, :] = jnp.zeros((block, target.shape[1]), target.dtype)


def stacked(ref, h):
    return jnp.concatenate([ref[:, lanes(h, GROUPS * HD, r * HD, HD)] for r in range(GROUPS)], axis=0)


def for_each_length(live_rows, doc_rows, process):
    lengths = [doc_rows // STEPS * (k + 1) for k in range(STEPS)]
    for low, length in zip([0] + lengths, lengths):

        @pl.when((live_rows > low) & (live_rows <= length))
        def _(length=length):
            process(length)


def query_kernel(
    first_head,
    n_done,
    place,
    q_ref,
    go_ref,
    leaf_ref,
    bias_ref,
    final_ref,
    keys_ref,
    dlog_ref,
    *rest,
):
    dq_ref, dleaf_ref, prob, dlog = rest[n_done:]
    h = first_head + pl.program_id(0)
    rows = q_ref.shape[0]
    leaf_keys = leaf_ref[:, lanes(h, 2 * HD, 0, HD)]
    leaf_values = leaf_ref[:, lanes(h, 2 * HD, HD, HD)]
    leaf_turned = jnp.transpose(leaf_keys)
    for r in range(GROUPS):
        cols = lanes(h, GROUPS * HD, r * HD, HD)
        logit = dot(leaf_keys, q_ref[:, cols], NT) + bias_ref[...]
        probability = weights(logit, final_ref[h, 0, r : r + 1, :]) * final_ref[h, 1, r : r + 1, :]
        grad_prob = dot(leaf_values, go_ref[:, cols], NT)
        grad_logit = probability * (grad_prob - final_ref[h, 2, r : r + 1, :])
        prob[:, r * rows : (r + 1) * rows] = probability.astype(jnp.bfloat16)
        dlog[:, r * rows : (r + 1) * rows] = grad_logit.astype(jnp.bfloat16)
    grad_key = dot(dlog[...], stacked(q_ref, h), NN) * SCALE
    dleaf_ref[:, :HD] = grad_key.astype(jnp.bfloat16)
    dleaf_ref[:, HD:] = dot(prob[...], stacked(go_ref, h), NN).astype(jnp.bfloat16)

    def process(length):
        doc_turned = jnp.transpose(keys_ref[:length, lanes(h, 2 * HD, 0, HD)])
        for r in range(GROUPS):
            part = slice(r * rows, (r + 1) * rows)
            dq = dot(leaf_turned, dlog[:, part], NN)
            dq = dq + dot(doc_turned, dlog_ref[h, :length, part], NN)
            dq_ref[:, r * HD : (r + 1) * HD] = jnp.transpose(dq * SCALE).astype(jnp.bfloat16)

    for_each_length(place[place.shape[0] - 1], keys_ref.shape[0], process)


IN_VMEM = pl.BlockSpec(memory_space=pltpu.VMEM)
IN_SMEM = pl.BlockSpec(memory_space=pltpu.SMEM)
PARAMS = pltpu.CompilerParams(vmem_limit_bytes=16 * 1024 * 1024)


def shape(dims, dtype):
    return jax.ShapeDtypeStruct(dims, dtype)


def cost(queries, pairs, matmuls, extra):
    return pl.CostEstimate(
        flops=2 * HD * pairs * queries * matmuls,
        bytes_accessed=4 * HD * queries + extra,
        transcendentals=pairs * queries,
    )


def prepare(tok_size, block, block_parent, leaf_block, leaf_seg):
    rows = leaf_seg.shape[1]
    return pl.pallas_call(
        functools.partial(prepare_kernel, tok_size, block),
        out_shape=(shape((rows, rows), jnp.float32), shape((tok_size + 1,), jnp.int32)),
        in_specs=[IN_SMEM, IN_SMEM, IN_VMEM],
        out_specs=(IN_VMEM, IN_SMEM),
        scratch_shapes=[pltpu.SMEM((tok_size,), jnp.int32)],
        compiler_params=PARAMS,
        cost_estimate=cost(16 * rows, rows, 1, 16 * 1024 * 1024),
        name="prepare",
    )(block_parent, leaf_block, leaf_seg)


def leaf_stats(bias, query, grad_out, leaf_kv):
    rows = query.shape[0]
    heads = leaf_kv.shape[1] // (2 * HD)
    return pl.pallas_call(
        leaf_kernel,
        out_shape=shape((heads, 3, 8, rows), jnp.float32),
        in_specs=[IN_VMEM] * 4,
        out_specs=IN_VMEM,
        compiler_params=PARAMS,
        cost_estimate=cost(rows * heads * GROUPS, rows, 4, 0),
        name="leaf_stats",
    )(bias, query, grad_out, leaf_kv)


def doc_grads(tok_size, place, query, grad_out, near, far, stats):
    rows = query.shape[0]
    heads = stats.shape[0]
    doc_rows = 2 * near.shape[0]
    return pl.pallas_call(
        functools.partial(doc_kernel, tok_size),
        out_shape=(
            shape(near.shape, jnp.float32),
            shape(far.shape, jnp.bfloat16),
            shape(stats.shape, jnp.float32),
            shape((doc_rows, near.shape[1]), jnp.bfloat16),
            shape((heads, doc_rows, GROUPS * rows), jnp.bfloat16),
        ),
        in_specs=[IN_SMEM] + [IN_VMEM] * 5,
        out_specs=(IN_VMEM,) * 5,
        scratch_shapes=[
            pltpu.VMEM((doc_rows, GROUPS * rows), jnp.bfloat16),
            pltpu.VMEM((doc_rows, near.shape[1]), jnp.float32),
        ],
        compiler_params=PARAMS,
        cost_estimate=cost(rows * heads * GROUPS, doc_rows, 4, 0),
        name="doc_grads",
    )(place, query, grad_out, near, far, stats)


def query_grads(first, heads, done, place, query, grad_out, leaf_kv, bias, final, keys, dlog):
    rows = query.shape[0]
    wide = pl.BlockSpec((rows, GROUPS * HD), lambda g: (0, first + g))
    pair = pl.BlockSpec((rows, 2 * HD), lambda g: (0, first + g))
    return pl.pallas_call(
        functools.partial(query_kernel, first, len(done)),
        out_shape=(shape(query.shape, jnp.bfloat16), shape(leaf_kv.shape, jnp.bfloat16)),
        grid=(heads,),
        in_specs=[IN_SMEM] + [IN_VMEM] * 7 + [pl.BlockSpec(memory_space=pl.ANY)] * len(done),
        out_specs=(wide, pair),
        input_output_aliases={8 + i: i for i in range(len(done))},
        scratch_shapes=[pltpu.VMEM((rows, GROUPS * rows), jnp.bfloat16)] * 2,
        compiler_params=PARAMS,
        cost_estimate=cost(rows * heads * GROUPS, rows, 8, 0),
        name="query_grads",
    )(place, query, grad_out, leaf_kv, bias, final, keys, dlog, *done)


def body(tok_size, head_size, query, leaf_kv, doc_kv, grad_out, block_parent, leaf_block, leaf_seg):
    width = leaf_kv.shape[1]
    block = doc_kv.shape[0] * head_size
    orders = hop_orders(tok_size)
    rounds = len(orders[0])
    head = lax.axis_index("head")
    swap_head = [(0, 1), (1, 0)]

    def exchange(value, r):
        return lax.ppermute(value, "tok", [(i, i ^ orders[i % 2][r]) for i in range(tok_size)])

    def swap_core(value):
        return lax.ppermute(value, "tok", [(i, i ^ 1) for i in range(tok_size)])

    if head_size == 2:
        arrived = lax.ppermute(doc_kv, "head", swap_head)
        own = lax.dynamic_slice_in_dim(doc_kv, head * width, width, 1)
        arrived, own = lax.optimization_barrier((arrived, own))
        arrived = lax.dynamic_slice_in_dim(arrived, head * width, width, 1)
        held = jnp.concatenate([own, arrived], axis=0)
    else:
        held = lax.all_to_all(doc_kv, "head", split_axis=1, concat_axis=0, tiled=True)
    resident = (query, grad_out, leaf_kv)
    early_round = max(0, rounds - 2)
    for r in range(rounds):
        if r == early_round:
            held, leaf_seg = lax.optimization_barrier((held, leaf_seg))
        if r == rounds - 1:
            held, bias = lax.optimization_barrier((held, bias))
        arrived = exchange(held, r)
        if r == early_round:
            early = prepare(tok_size, block, block_parent, leaf_block, leaf_seg)
            arrived, (bias, place) = lax.optimization_barrier((arrived, early))
        if r == rounds - 1:
            arrived, stats = lax.optimization_barrier((arrived, leaf_stats(bias, *resident)))
        held = jnp.concatenate([held, arrived], axis=0)
    crossed = swap_core(held)

    total, sent, final, keys, dlog = doc_grads(tok_size, place, *resident[:2], held, crossed, stats)
    total = total + swap_core(sent).astype(jnp.float32)
    heads = final.shape[0]
    parts = [2, 1, 1] if heads == 4 else [heads]
    done = []
    for step in range(rounds):
        kept = total.shape[0] // 2
        leaving = total[kept:].astype(jnp.bfloat16)
        if step < len(parts):
            leaving, final = lax.optimization_barrier((leaving, final))
        arrived = exchange(leaving, rounds - 1 - step)
        if step < len(parts):
            first = sum(parts[:step])
            done = query_grads(
                first, parts[step], done, place, *resident, bias, final, keys, dlog
            )
            arrived, done = lax.optimization_barrier((arrived, done))
        total = total[:kept] + arrived.astype(jnp.float32)
    query_grad, leaf_grad = done
    total = total.astype(jnp.bfloat16)
    if head_size == 2:
        kept = total.shape[0] // 2
        mine = total[:kept]
        arrived = lax.ppermute(total[kept:], "head", swap_head)
        doc_grad = jnp.where(
            head == 0,
            jnp.concatenate([mine, arrived], axis=1),
            jnp.concatenate([arrived, mine], axis=1),
        )
    else:
        doc_grad = lax.all_to_all(total, "head", split_axis=0, concat_axis=1, tiled=True)
    return query_grad, leaf_grad, doc_grad


def solution(mesh):
    placed = (
        P("tok", "head"),
        P("tok", "head"),
        P(("tok", "head"), None),
        P("tok", "head"),
        P(),
        P(),
        P("tok", None),
    )
    return jax.shard_map(
        functools.partial(body, mesh.shape["tok"], mesh.shape["head"]),
        mesh=mesh,
        in_specs=placed,
        out_specs=(P("tok", "head"), P("tok", "head"), P(("tok", "head"), None)),
        check_vma=False,
    )
```

```python
import functools

import jax
import jax.numpy as jnp
from jax import lax
from jax.experimental import pallas as pl
from jax.experimental.pallas import tpu as pltpu
from jax.sharding import PartitionSpec as P

QH = 40
KVH = 8
HD = 128
GROUPS = QH // KVH
SCALE = HD ** (-0.5)
LOG2E = 1.4426950408889634
HIDDEN = -1e30
STEPS = 8
NN = (((1,), (0,)), ((), ()))
NT = (((1,), (1,)), ((), ()))
TN = (((0,), (0,)), ((), ()))


def hop_orders(tok_size):
    masks = [1 << b for b in range(tok_size.bit_length() - 1)]
    far = masks[:0:-1]
    other = far if len(far) < 3 else far[:-2] + [far[-1], far[-2]]
    return far, other


def dot(a, b, dims):
    return lax.dot_general(a, b, dims, preferred_element_type=jnp.float32)


def weights(logit, top):
    return jnp.exp2((logit - top) * (SCALE * LOG2E))


def lanes(h, width, first, size):
    return pl.ds(pl.multiple_of(h * width + first, HD), size)


def prepare_kernel(tok_size, block, tables, seg_ref, bias_ref, place_ref, seen):
    rows = bias_ref.shape[0]
    me = lax.axis_index("tok")

    def clear(i, carry):
        seen[i] = 0
        return carry

    lax.fori_loop(0, tok_size, clear, 0)

    def climb(i, node):
        seen[node] = 1
        return tables[node]

    lax.fori_loop(0, tok_size, climb, tables[tok_size + me])
    masks = hop_orders(tok_size)[0] + [1]
    total = jnp.int32(0)
    for position in range(tok_size):
        owner = me ^ sum(m for r, m in enumerate(masks) if position >> r & 1)
        visible = seen[owner]
        place_ref[position] = jnp.where(visible == 1, total, -1)
        total = total + visible
    place_ref[tok_size] = total * block

    across = jnp.broadcast_to(seg_ref[...].astype(jnp.float32), (rows, rows))
    down = jnp.transpose(across)
    key = lax.broadcasted_iota(jnp.int32, (rows, rows), 0)
    asker = lax.broadcasted_iota(jnp.int32, (rows, rows), 1)
    bias_ref[...] = jnp.where((across == down) & (key <= asker), 0.0, HIDDEN)


def leaf_kernel(bias_ref, q_ref, go_ref, leaf_ref, stats_ref):
    def one_head(h, carry):
        leaf_keys = leaf_ref[:, lanes(h, 2 * HD, 0, HD)]
        leaf_values = leaf_ref[:, lanes(h, 2 * HD, HD, HD)]
        for r in range(GROUPS):
            cols = lanes(h, GROUPS * HD, r * HD, HD)
            logit = dot(leaf_keys, q_ref[:, cols], NT) + bias_ref[...]
            top = jnp.max(logit, axis=0, keepdims=True)
            weight = weights(logit, top)
            grad_prob = dot(leaf_values, go_ref[:, cols], NT)
            stats_ref[h, 0, r : r + 1, :] = top
            stats_ref[h, 1, r : r + 1, :] = jnp.sum(weight, axis=0, keepdims=True)
            stats_ref[h, 2, r : r + 1, :] = jnp.sum(weight * grad_prob, axis=0, keepdims=True)
        return carry

    lax.fori_loop(0, stats_ref.shape[0], one_head, 0)


def doc_kernel(
    tok_size,
    place,
    q_ref,
    go_ref,
    near_ref,
    far_ref,
    stats_ref,
    dnear_ref,
    dfar_ref,
    final_ref,
    keys_ref,
    dlog_ref,
    prob,
    grads,
):
    rows = q_ref.shape[0]
    heads = stats_ref.shape[0]
    doc_rows = near_ref.shape[0] + far_ref.shape[0]
    half = tok_size // 2
    block = doc_rows // tok_size
    live_rows = place[tok_size]
    for spare in range(doc_rows // STEPS // block - 1):

        @pl.when(live_rows + spare * block < doc_rows)
        def _(spare=spare):
            row = pl.multiple_of(live_rows + spare * block, block)
            keys_ref[pl.ds(row, block), :] = jnp.zeros((block, keys_ref.shape[1]), keys_ref.dtype)

    for position in range(tok_size):
        source = near_ref if position < half else far_ref
        first = (position % half) * block
        slot = place[position]

        @pl.when(slot >= 0)
        def _(source=source, first=first, slot=slot):
            row = pl.multiple_of(slot * block, block)
            keys_ref[pl.ds(row, block), :] = source[first : first + block, :]

    def process(length):
        body_rows = length - doc_rows // STEPS
        row = body_rows + lax.broadcasted_iota(jnp.int32, (doc_rows // STEPS, 1), 0)
        live = row < live_rows

        def one_head(h, carry):
            doc_keys = keys_ref[:length, lanes(h, 2 * HD, 0, HD)]
            doc_values = keys_ref[:length, lanes(h, 2 * HD, HD, HD)]
            for r in range(GROUPS):
                cols = lanes(h, GROUPS * HD, r * HD, HD)
                logit = dot(doc_keys, q_ref[:, cols], NT)
                tail = jnp.where(live, logit[body_rows:], HIDDEN)
                logit = jnp.concatenate([logit[:body_rows], tail], axis=0) if body_rows else tail
                leaf_top = stats_ref[h, 0, r : r + 1, :]
                top = jnp.maximum(leaf_top, jnp.max(logit, axis=0, keepdims=True))
                shrink = weights(leaf_top, top)
                weight = weights(logit, top)
                leaf_sum = stats_ref[h, 1, r : r + 1, :] * shrink
                leaf_dot = stats_ref[h, 2, r : r + 1, :] * shrink
                inverse = 1.0 / (leaf_sum + jnp.sum(weight, axis=0, keepdims=True))
                grad_prob = dot(doc_values, go_ref[:, cols], NT)
                grad_dot = leaf_dot + jnp.sum(weight * grad_prob, axis=0, keepdims=True)
                grad_dot = grad_dot * inverse
                probability = weight * inverse
                prob[:length, r * rows : (r + 1) * rows] = probability.astype(jnp.bfloat16)
                grad_logit = (probability * (grad_prob - grad_dot)).astype(jnp.bfloat16)
                dlog_ref[h, :length, r * rows : (r + 1) * rows] = grad_logit
                final_ref[h, 0, r : r + 1, :] = top
                final_ref[h, 1, r : r + 1, :] = inverse
                final_ref[h, 2, r : r + 1, :] = grad_dot
            q_all = stacked(q_ref, h)
            go_all = stacked(go_ref, h)
            grad_key = dot(dlog_ref[h, :length, :], q_all, NN) * SCALE
            grads[:length, lanes(h, 2 * HD, 0, HD)] = grad_key
            grads[:length, lanes(h, 2 * HD, HD, HD)] = dot(prob[:length, :], go_all, NN)
            return carry

        lax.fori_loop(0, heads, one_head, 0)

    for_each_length(live_rows, doc_rows, process)

    gathered, other = hop_orders(tok_size)
    core = lax.rem(lax.axis_index("tok"), 2)
    for position in range(tok_size):
        target = dnear_ref if position < half else dfar_ref
        local = position % half
        moved = sum(1 << other.index(m) for r, m in enumerate(gathered) if local >> r & 1)
        at = jnp.where(core == (1 if position < half else 0), moved, local)
        slot = place[position]
        leaving = pl.ds(pl.multiple_of(at * block, block), block)

        @pl.when(slot >= 0)
        def _(target=target, leaving=leaving, slot=slot):
            row = pl.multiple_of(slot * block, block)
            target[leaving, :] = grads[pl.ds(row, block), :].astype(target.dtype)

        @pl.when(slot < 0)
        def _(target=target, leaving=leaving):
            target[leaving, :] = jnp.zeros((block, target.shape[1]), target.dtype)


def stacked(ref, h):
    return jnp.concatenate([ref[:, lanes(h, GROUPS * HD, r * HD, HD)] for r in range(GROUPS)], axis=0)


def for_each_length(live_rows, doc_rows, process):
    lengths = [doc_rows // STEPS * (k + 1) for k in range(STEPS)]
    for low, length in zip([0] + lengths, lengths):

        @pl.when((live_rows > low) & (live_rows <= length))
        def _(length=length):
            process(length)


def query_kernel(
    first_head,
    n_done,
    place,
    q_ref,
    go_ref,
    leaf_ref,
    bias_ref,
    final_ref,
    keys_ref,
    dlog_ref,
    *rest,
):
    dq_ref, dleaf_ref, prob, dlog = rest[n_done:]
    h = first_head + pl.program_id(0)
    rows = q_ref.shape[0]
    leaf_keys = leaf_ref[:, lanes(h, 2 * HD, 0, HD)]
    leaf_values = leaf_ref[:, lanes(h, 2 * HD, HD, HD)]
    leaf_turned = jnp.transpose(leaf_keys)
    for r in range(GROUPS):
        cols = lanes(h, GROUPS * HD, r * HD, HD)
        logit = dot(leaf_keys, q_ref[:, cols], NT) + bias_ref[...]
        probability = weights(logit, final_ref[h, 0, r : r + 1, :]) * final_ref[h, 1, r : r + 1, :]
        grad_prob = dot(leaf_values, go_ref[:, cols], NT)
        grad_logit = probability * (grad_prob - final_ref[h, 2, r : r + 1, :])
        prob[:, r * rows : (r + 1) * rows] = probability.astype(jnp.bfloat16)
        dlog[:, r * rows : (r + 1) * rows] = grad_logit.astype(jnp.bfloat16)
    grad_key = dot(dlog[...], stacked(q_ref, h), NN) * SCALE
    dleaf_ref[:, :HD] = grad_key.astype(jnp.bfloat16)
    dleaf_ref[:, HD:] = dot(prob[...], stacked(go_ref, h), NN).astype(jnp.bfloat16)

    def process(length):
        doc_turned = jnp.transpose(keys_ref[:length, lanes(h, 2 * HD, 0, HD)])
        for r in range(GROUPS):
            part = slice(r * rows, (r + 1) * rows)
            dq = dot(leaf_turned, dlog[:, part], NN)
            dq = dq + dot(doc_turned, dlog_ref[h, :length, part], NN)
            dq_ref[:, r * HD : (r + 1) * HD] = jnp.transpose(dq * SCALE).astype(jnp.bfloat16)

    for_each_length(place[place.shape[0] - 1], keys_ref.shape[0], process)


IN_VMEM = pl.BlockSpec(memory_space=pltpu.VMEM)
IN_SMEM = pl.BlockSpec(memory_space=pltpu.SMEM)
PARAMS = pltpu.CompilerParams(vmem_limit_bytes=16 * 1024 * 1024)


def shape(dims, dtype):
    return jax.ShapeDtypeStruct(dims, dtype)


def cost(queries, pairs, matmuls, extra):
    return pl.CostEstimate(
        flops=2 * HD * pairs * queries * matmuls,
        bytes_accessed=4 * HD * queries + extra,
        transcendentals=pairs * queries,
    )


def prepare(tok_size, block, tables, leaf_seg):
    rows = leaf_seg.shape[1]
    return pl.pallas_call(
        functools.partial(prepare_kernel, tok_size, block),
        out_shape=(shape((rows, rows), jnp.float32), shape((tok_size + 1,), jnp.int32)),
        in_specs=[IN_SMEM, IN_VMEM],
        out_specs=(IN_VMEM, IN_SMEM),
        scratch_shapes=[pltpu.SMEM((tok_size,), jnp.int32)],
        compiler_params=PARAMS,
        cost_estimate=cost(16 * rows, rows, 1, 16 * 1024 * 1024),
        name="prepare",
    )(tables, leaf_seg)


def leaf_stats(bias, query, grad_out, leaf_kv):
    rows = query.shape[0]
    heads = leaf_kv.shape[1] // (2 * HD)
    return pl.pallas_call(
        leaf_kernel,
        out_shape=shape((heads, 3, 8, rows), jnp.float32),
        in_specs=[IN_VMEM] * 4,
        out_specs=IN_VMEM,
        compiler_params=PARAMS,
        cost_estimate=cost(rows * heads * GROUPS, rows, 4, 0),
        name="leaf_stats",
    )(bias, query, grad_out, leaf_kv)


def doc_grads(tok_size, place, query, grad_out, near, far, stats):
    rows = query.shape[0]
    heads = stats.shape[0]
    doc_rows = 2 * near.shape[0]
    return pl.pallas_call(
        functools.partial(doc_kernel, tok_size),
        out_shape=(
            shape(near.shape, jnp.float32),
            shape(far.shape, jnp.bfloat16),
            shape(stats.shape, jnp.float32),
            shape((doc_rows, near.shape[1]), jnp.bfloat16),
            shape((heads, doc_rows, GROUPS * rows), jnp.bfloat16),
        ),
        in_specs=[IN_SMEM] + [IN_VMEM] * 5,
        out_specs=(IN_VMEM,) * 5,
        scratch_shapes=[
            pltpu.VMEM((doc_rows, GROUPS * rows), jnp.bfloat16),
            pltpu.VMEM((doc_rows, near.shape[1]), jnp.float32),
        ],
        compiler_params=PARAMS,
        cost_estimate=cost(rows * heads * GROUPS, doc_rows, 4, 0),
        name="doc_grads",
    )(place, query, grad_out, near, far, stats)


def query_grads(first, heads, done, place, query, grad_out, leaf_kv, bias, final, keys, dlog):
    rows = query.shape[0]
    wide = pl.BlockSpec((rows, GROUPS * HD), lambda g: (0, first + g))
    pair = pl.BlockSpec((rows, 2 * HD), lambda g: (0, first + g))
    return pl.pallas_call(
        functools.partial(query_kernel, first, len(done)),
        out_shape=(shape(query.shape, jnp.bfloat16), shape(leaf_kv.shape, jnp.bfloat16)),
        grid=(heads,),
        in_specs=[IN_SMEM] + [IN_VMEM] * 7 + [pl.BlockSpec(memory_space=pl.ANY)] * len(done),
        out_specs=(wide, pair),
        input_output_aliases={8 + i: i for i in range(len(done))},
        scratch_shapes=[pltpu.VMEM((rows, GROUPS * rows), jnp.bfloat16)] * 2,
        compiler_params=PARAMS,
        cost_estimate=cost(rows * heads * GROUPS, rows, 8, 0),
        name="query_grads",
    )(place, query, grad_out, leaf_kv, bias, final, keys, dlog, *done)


def body(tok_size, head_size, query, leaf_kv, doc_kv, grad_out, block_parent, leaf_block, leaf_seg):
    width = leaf_kv.shape[1]
    block = doc_kv.shape[0] * head_size
    orders = hop_orders(tok_size)
    rounds = len(orders[0])
    head = lax.axis_index("head")
    swap_head = [(0, 1), (1, 0)]

    def exchange(value, even, odd):
        pairs = [(i, i ^ (odd if i % 2 else even)) for i in range(tok_size)]
        return lax.ppermute(value, "tok", pairs)

    tables = jnp.concatenate([block_parent, leaf_block])
    if head_size == 2:
        arrived = lax.ppermute(doc_kv, "head", swap_head)
        own = lax.dynamic_slice_in_dim(doc_kv, head * width, width, 1)
        arrived, own, tables = lax.optimization_barrier((arrived, own, tables))
        arrived = lax.dynamic_slice_in_dim(arrived, head * width, width, 1)
        held = jnp.concatenate([own, arrived], axis=0)
    else:
        held = lax.all_to_all(doc_kv, "head", split_axis=1, concat_axis=0, tiled=True)
    resident = (query, grad_out, leaf_kv)
    early_round = max(0, rounds - 2)
    for r in range(rounds):
        if r == early_round:
            held, leaf_seg = lax.optimization_barrier((held, leaf_seg))
        if r == rounds - 1:
            held, bias = lax.optimization_barrier((held, bias))
        arrived = exchange(held, orders[0][r], orders[0][r])
        if r == early_round:
            early = prepare(tok_size, block, tables, leaf_seg)
            arrived, (bias, place) = lax.optimization_barrier((arrived, early))
        if r == rounds - 1:
            arrived, stats = lax.optimization_barrier((arrived, leaf_stats(bias, *resident)))
        held = jnp.concatenate([held, arrived], axis=0)
    crossed = exchange(held, 1, 1)

    total, sent, final, keys, dlog = doc_grads(tok_size, place, *resident[:2], held, crossed, stats)
    total = total + exchange(sent, 1, 1).astype(jnp.float32)
    heads = final.shape[0]
    parts = [2, 1, 1] if heads == 4 else [heads]
    done = []
    for step in range(rounds):
        kept = total.shape[0] // 2
        leaving = total[kept:].astype(jnp.bfloat16)
        if step < len(parts):
            leaving, final = lax.optimization_barrier((leaving, final))
        arrived = exchange(leaving, *(order[rounds - 1 - step] for order in orders))
        if step < len(parts):
            first = sum(parts[:step])
            done = query_grads(
                first, parts[step], done, place, *resident, bias, final, keys, dlog
            )
            arrived, done = lax.optimization_barrier((arrived, done))
        total = total[:kept] + arrived.astype(jnp.float32)
    query_grad, leaf_grad = done
    total = total.astype(jnp.bfloat16)
    if head_size == 2:
        kept = total.shape[0] // 2
        mine = total[:kept]
        arrived = lax.ppermute(total[kept:], "head", swap_head)
        doc_grad = jnp.where(
            head == 0,
            jnp.concatenate([mine, arrived], axis=1),
            jnp.concatenate([arrived, mine], axis=1),
        )
    else:
        doc_grad = lax.all_to_all(total, "head", split_axis=0, concat_axis=1, tiled=True)
    return query_grad, leaf_grad, doc_grad


def solution(mesh):
    placed = (
        P("tok", "head"),
        P("tok", "head"),
        P(("tok", "head"), None),
        P("tok", "head"),
        P(),
        P(),
        P("tok", None),
    )
    return jax.shard_map(
        functools.partial(body, mesh.shape["tok"], mesh.shape["head"]),
        mesh=mesh,
        in_specs=placed,
        out_specs=(P("tok", "head"), P("tok", "head"), P(("tok", "head"), None)),
        check_vma=False,
    )
```
